32 devices in a mesh: gen: 8 (over y, x, core), tp: 4 (over z).
Axes of the slice: x: 2, y: 2, z: 4, core: 2. Of those that a mesh axis runs over, the one named last changes fastest.
Arguments:
- hidden_in: bfloat16 [4, 16, 8192], P(None, 'gen'), may hold values from -6 to 6
- norm_gain: bfloat16 [8192], replicated, may hold values from 0.099609375 to 1.8984375
- w_query: bfloat16 [8192, 4096], P(('gen', 'tp')), may hold values from -0.0625 to 0.0625
- key_weight_matrix: bfloat16 [8192, 1024], P(('gen', 'tp')), may hold values from -0.0625 to 0.0625
- value_weight_matrix: bfloat16 [8192, 1024], P(('gen', 'tp')), may hold values from -0.0625 to 0.0625
- bias_query: bfloat16 [4096], P('tp'), may hold values from -3 to 3
- key_bias_vector: bfloat16 [1024], P('tp'), may hold values from -3 to 3
- value_bias_vector: bfloat16 [1024], P('tp'), may hold values from -3 to 3
- w_out: bfloat16 [4096, 8192], P(None, ('gen', 'tp')), may hold values from -0.09375 to 0.09375
- key_cache: bfloat16 [16, 8, 16384, 128], P('gen', 'tp'), may hold values from -400 to 400
- value_cache: bfloat16 [16, 8, 16384, 128], P('gen', 'tp'), may hold values from -16 to 16
- lengths: int32 [16], P('gen'), may hold values from 1 to 16384
- finished: int32 [16], P('gen'), may hold values 0 or 1
Outputs:
- layer_out: bfloat16 [4, 16, 8192], P(None, 'gen')
The draws below stay inside these ranges and needn't reach their ends.
All inputs are finite; a program needn't handle non-finite values. No bound on the sum of `finished` on one device may be relied on, other than what follows from the above.
Results may differ from the reference program's by a relative error of at most 0.012.
Values may be sent and summed in bfloat16 or wider, within the bound.
No kernel may reach another device: no remote copies, remote signals or barrier semaphores. Data moves between devices by JAX's collectives and lax.ppermute only.
A program may use at most 128 MiB of HBM per device.

```python
import math
import jax
import jax.numpy as jnp
from jax import lax

MODEL_DIM = 8192
HQ = 32
KEY_HEADS = 8
HEAD_SIZE = 128
QUERY_GROUP = 4
CACHE_SLOTS = 16384
DECODE_STEPS = 4
ROLLOUT_ROWS = 16


def draw_key_cache(key, part):
    first_term = jax.random.fold_in(jax.random.fold_in(key, 17), 0)
    base_values = jax.random.normal(first_term, (ROLLOUT_ROWS, KEY_HEADS, CACHE_SLOTS, HEAD_SIZE), jnp.float32) * 1.8
    return jnp.clip(base_values, -400.0, 400.0).astype(jnp.bfloat16)


def draw_value_cache(key, part):
    first_term, second_term = jax.random.split(jax.random.fold_in(key, 29), 2)
    center_point = jax.random.normal(first_term, (ROLLOUT_ROWS, KEY_HEADS, 1, HEAD_SIZE), jnp.float32)
    rough_values = jax.random.normal(second_term, (ROLLOUT_ROWS, KEY_HEADS, CACHE_SLOTS, HEAD_SIZE), jnp.float32)
    values = center_point + rough_values
    return jnp.clip(values, -16.0, 16.0).astype(jnp.bfloat16)


def set_ends(drawn, stream_key, smallest, largest):
    dims = drawn.shape
    spot = [jax.random.randint(jax.random.fold_in(stream_key, axis), (), 0, dims[axis]) for axis in range(len(dims))]
    drawn = drawn.at[tuple(spot)].set(smallest)
    longest = dims.index(max(dims))
    spot[longest] = (spot[longest] + 1) % dims[longest]
    return drawn.at[tuple(spot)].set(largest)


def steps_of(key, dims, cuts, smallest, largest):
    def one(position, parts):
        steps = jax.random.uniform(jax.random.fold_in(jax.random.fold_in(key, 6), position), (parts,), jnp.float32, smallest / len(cuts), largest / len(cuts))
        return jnp.repeat(jnp.exp(steps), dims[position] // parts).reshape((-1,) + (1,) * (len(dims) - position - 1))

    factor_of = one(*cuts[0])
    for cut in cuts[1:]:
        factor_of = factor_of * one(*cut)
    return factor_of


def normal_values(own_key, dims, deviation, reach, cuts=(), kind=jnp.bfloat16):
    loudness = steps_of(own_key, dims, cuts, -0.22, 0.18) if cuts else 1.0
    array = jax.random.normal(own_key, dims, jnp.float32) * deviation * loudness
    return jnp.minimum(jnp.maximum(array, -reach), reach).astype(kind)


def setup_inputs(seed: int = 0) -> dict:
    key_list = jax.random.split(jax.random.key(seed), 14)
    hidden_in = normal_values(key_list[0], (DECODE_STEPS, ROLLOUT_ROWS, MODEL_DIM), 1.0, 6.0, ((1, 8),))
    norm_gain = jnp.clip(1.0 + 0.18 * jax.random.normal(key_list[1], (MODEL_DIM,), jnp.float32), 0.099609375, 1.8984375).astype(jnp.bfloat16)
    w_query = normal_values(key_list[2], (MODEL_DIM, HQ * HEAD_SIZE), MODEL_DIM ** -0.5, 0.0625, ((0, 32),))
    key_weight_matrix = normal_values(key_list[3], (MODEL_DIM, KEY_HEADS * HEAD_SIZE), MODEL_DIM ** -0.5, 0.0625, ((0, 32),))
    value_weight_matrix = normal_values(key_list[4], (MODEL_DIM, KEY_HEADS * HEAD_SIZE), MODEL_DIM ** -0.5, 0.0625, ((0, 32),))
    bias_query = normal_values(key_list[5], (HQ * HEAD_SIZE,), 0.5, 3.0, ((0, 4),))
    key_bias_vector = normal_values(key_list[6], (KEY_HEADS * HEAD_SIZE,), 0.5, 3.0, ((0, 4),))
    value_bias_vector = normal_values(key_list[7], (KEY_HEADS * HEAD_SIZE,), 0.5, 3.0, ((0, 4),))
    w_out = normal_values(key_list[8], (HQ * HEAD_SIZE, MODEL_DIM), (HQ * HEAD_SIZE) ** -0.5, 0.09375, ((1, 32),))
    key_cache = draw_key_cache(jax.random.fold_in(key_list[13], 71), 0)
    value_cache = draw_value_cache(jax.random.fold_in(key_list[13], 71), 0)
    lengths = set_ends(jax.random.randint(key_list[11], (ROLLOUT_ROWS,), 1, CACHE_SLOTS + 1), jax.random.fold_in(key_list[11], 1), 1, CACHE_SLOTS).astype(jnp.int32)
    finished = set_ends((jax.random.randint(key_list[12], (ROLLOUT_ROWS,), 0, 4) < 1).astype(jnp.int32), jax.random.fold_in(key_list[12], 1), 0, 1)
    return dict(hidden_in=hidden_in, norm_gain=norm_gain, w_query=w_query, key_weight_matrix=key_weight_matrix, value_weight_matrix=value_weight_matrix, bias_query=bias_query, key_bias_vector=key_bias_vector, value_bias_vector=value_bias_vector, w_out=w_out, key_cache=key_cache, value_cache=value_cache, lengths=lengths, finished=finished)


norm_eps = 1e-06
rope_base = 1000000.0
masked_score = -1e+30

def apply_rotation(values, token_positions):
    half_dim = values.shape[-1] // 2
    pair_index = jnp.arange(half_dim).astype(jnp.float32)
    frequency = jnp.exp(pair_index * (-2.0 * math.log(rope_base) / values.shape[-1]))
    angles = token_positions[..., None] * frequency
    lower_half = values[..., :half_dim]
    upper_half = values[..., half_dim:]
    cosine = jnp.cos(angles)
    sine = jnp.sin(angles)
    return jnp.concatenate([lower_half * cosine - upper_half * sine, upper_half * cosine + lower_half * sine], axis=-1)

def reference(hidden_in, norm_gain, w_query, key_weight_matrix, value_weight_matrix, bias_query, key_bias_vector, value_bias_vector, w_out, key_cache, value_cache, lengths, finished):
    widened = hidden_in.astype(jnp.float32)
    normed = widened * lax.rsqrt(lax.optimization_barrier(jnp.mean(widened * widened, axis=-1, keepdims=True)) + norm_eps) * norm_gain.astype(jnp.float32)
    flattened = normed.astype(jnp.bfloat16).reshape(DECODE_STEPS * ROLLOUT_ROWS, MODEL_DIM)
    queries = jnp.dot(flattened, w_query, preferred_element_type=jnp.float32) + bias_query.astype(jnp.float32)
    new_key_rows = jnp.dot(flattened, key_weight_matrix, preferred_element_type=jnp.float32) + key_bias_vector.astype(jnp.float32)
    fresh_value_rows = jnp.dot(flattened, value_weight_matrix, preferred_element_type=jnp.float32) + value_bias_vector.astype(jnp.float32)
    token_positions = (lengths[None, :] + jnp.arange(DECODE_STEPS, dtype=jnp.int32)[:, None]).astype(jnp.float32)[:, :, None]
    rot_query = apply_rotation(queries.reshape(DECODE_STEPS, ROLLOUT_ROWS, HQ, HEAD_SIZE), token_positions).astype(jnp.bfloat16)
    rotated_key = apply_rotation(new_key_rows.reshape(DECODE_STEPS, ROLLOUT_ROWS, KEY_HEADS, HEAD_SIZE), token_positions).astype(jnp.bfloat16)
    value_rows_new = fresh_value_rows.reshape(DECODE_STEPS, ROLLOUT_ROWS, KEY_HEADS, HEAD_SIZE).astype(jnp.bfloat16)
    score_scale = 1.0 / math.sqrt(HEAD_SIZE)
    allowed = jnp.arange(DECODE_STEPS)[None, :] <= jnp.arange(DECODE_STEPS)[:, None]

    def one_row(row_items):
        single_query_row, key_row, value_row, cache_keys, cache_values, length = row_items
        grouped_heads = single_query_row.reshape(DECODE_STEPS, KEY_HEADS, QUERY_GROUP, HEAD_SIZE).astype(jnp.float32)
        cache_scores = jnp.einsum('sjgd,jcd->sjgc', grouped_heads, cache_keys.astype(jnp.float32)) * score_scale
        inside = jnp.arange(CACHE_SLOTS) < length
        cache_scores = jnp.where(inside, cache_scores, masked_score)
        fresh_scores = jnp.einsum('sjgd,ujd->sjgu', grouped_heads, key_row.astype(jnp.float32)) * score_scale
        fresh_scores = jnp.where(allowed[:, None, None, :], fresh_scores, masked_score)
        scores = jnp.concatenate([cache_scores, fresh_scores], axis=-1)
        row_max = lax.optimization_barrier(jnp.max(scores, axis=-1, keepdims=True))
        weights = jnp.exp(scores - row_max)
        row_sum = lax.optimization_barrier(jnp.sum(weights, axis=-1))
        rounded = lax.optimization_barrier(weights.astype(jnp.bfloat16)).astype(jnp.float32)
        numerator = jnp.einsum('sjgc,jcd->sjgd', rounded[..., :CACHE_SLOTS], cache_values.astype(jnp.float32))
        numerator = numerator + jnp.einsum('sjgu,ujd->sjgd', rounded[..., CACHE_SLOTS:], value_row.astype(jnp.float32))
        return (numerator / row_sum[..., None]).astype(jnp.bfloat16).reshape(DECODE_STEPS, HQ * HEAD_SIZE)
    attended = lax.map(one_row, (jnp.transpose(rot_query, (1, 0, 2, 3)), jnp.transpose(rotated_key, (1, 0, 2, 3)), jnp.transpose(value_rows_new, (1, 0, 2, 3)), key_cache, value_cache, lengths))
    attended = jnp.transpose(attended, (1, 0, 2)).reshape(DECODE_STEPS * ROLLOUT_ROWS, HQ * HEAD_SIZE)
    projected = jnp.dot(attended, w_out, preferred_element_type=jnp.float32).reshape(DECODE_STEPS, ROLLOUT_ROWS, MODEL_DIM)
    layer_out = jnp.where(finished[None, :, None] != 0, widened, widened + projected)
    return layer_out.astype(jnp.bfloat16)
```

```python
import math

import jax
import jax.numpy as jnp
from jax import lax
from jax.experimental import pallas as pl
from jax.experimental.pallas import tpu as pltpu
from jax.sharding import Mesh
from jax.sharding import PartitionSpec as P

norm_eps = 1e-06
rope_base = 1000000.0
masked_score = -1e30
bf16 = jnp.bfloat16
f32 = jnp.float32


whole = pl.BlockSpec(memory_space=pltpu.VMEM)
scalars = pl.BlockSpec(memory_space=pltpu.SMEM)


def params(mib):
    return pltpu.CompilerParams(vmem_limit_bytes=mib << 20)


def in_vmem(array):
    return pltpu.with_memory_space_constraint(array, pltpu.VMEM)


def qkv_partials(columns, weights):
    cores, rows, width = columns.shape
    chips = lax.axis_size("chip")
    tp = lax.axis_size("tp")
    per = rows // chips
    sizes = [w.shape[1] // tp for w in weights[0]]
    total = sum(sizes)
    flat = [w for group in weights for w in group]

    def kernel(x_ref, *refs):
        out_ref = refs[-1]
        for t in range(tp):
            start = 0
            for i, size in enumerate(sizes):
                acc = None
                for c in range(cores):
                    w = refs[c * len(sizes) + i][:, t * size : (t + 1) * size]
                    part = jnp.dot(x_ref[c], w, preferred_element_type=f32)
                    acc = part if acc is None else acc + part
                acc = acc.astype(bf16)
                for n in range(chips):
                    out_ref[n * tp + t, :, start : start + size] = acc[n * per : (n + 1) * per]
                start += size

    flops = 2 * cores * rows * width * total * tp
    return pl.pallas_call(
        kernel,
        out_shape=jax.ShapeDtypeStruct((chips * tp, per, total), bf16),
        in_specs=[whole] * (1 + len(flat)),
        out_specs=whole,
        compiler_params=params(16),
        cost_estimate=pl.CostEstimate(
            flops=flops, bytes_accessed=2 * cores * width * total * tp, transcendentals=0
        ),
        name="qkv_partials",
    )(columns, *flat)


def attention(live, parts, scale, bias, cosine, sine, key_cache, value_cache, copies):
    sources, lines, total = parts.shape
    row_count, kv_heads, cache_len, head_dim = key_cache.shape
    steps = lines // row_count
    kv_width = kv_heads * head_dim
    q_width = total - 2 * kv_width
    heads = q_width // head_dim
    group = heads // kv_heads
    queries = group * steps
    block = min(cache_len, 2048)
    fresh = 8
    factor = math.log2(math.e) / math.sqrt(head_dim)

    def kernel(live_ref, p_ref, scale_ref, bias_ref, cos_ref, sin_ref, k_ref, v_ref, out_ref,
               q_scr, kn_scr, vn_scr, s_scr):
        x = p_ref[0].astype(f32)
        for i in range(1, sources):
            x = x + p_ref[i].astype(f32)
        x = x * scale_ref[:, 0:1] + bias_ref[...].astype(f32)
        cos = cos_ref[...]
        sin = sin_ref[...]

        def rotated(start):
            head = x[:, start : start + head_dim]
            return head * cos + pltpu.roll(head, head_dim // 2, 1) * sin

        kn_scr[...] = jnp.zeros_like(kn_scr)
        vn_scr[...] = jnp.zeros_like(vn_scr)
        for h in range(heads):
            q = rotated(h * head_dim)
            for r in range(row_count):
                g = h % group
                q_scr[r, h // group, g * steps : (g + 1) * steps, :] = q[r * steps : (r + 1) * steps]
        for j in range(kv_heads):
            k = rotated(q_width + j * head_dim)
            v = x[:, q_width + kv_width + j * head_dim : q_width + kv_width + (j + 1) * head_dim]
            for r in range(row_count):
                kn_scr[r, j, 0:steps, :] = k[r * steps : (r + 1) * steps]
                vn_scr[r, j, 0:steps, :] = v[r * steps : (r + 1) * steps]
        step_of = lax.broadcasted_iota(jnp.int32, (queries, fresh), 0) % steps
        allowed = lax.broadcasted_iota(jnp.int32, (queries, fresh), 1) <= step_of
        nt = (((1,), (1,)), ((), ()))
        for r in range(row_count):
            length = live_ref[r]
            blocks = (length + block - 1) // block
            qs = [q_scr[r, j].astype(bf16) for j in range(kv_heads)]

            def score(i, most):
                start = pl.multiple_of(i * block, block)
                place = start + lax.broadcasted_iota(jnp.int32, (queries, block), 1)
                inside = place < length
                out = []
                for j in range(kv_heads):
                    s = lax.dot_general(
                        qs[j], k_ref[r, j, pl.ds(start, block), :], nt, preferred_element_type=f32
                    )
                    s = jnp.where(inside, s, masked_score)
                    s_scr[j, :, pl.ds(start, block)] = s
                    top = most[j]
                    for b in range(block // 128):
                        top = jnp.maximum(top, s[:, b * 128 : (b + 1) * 128])
                    out.append(top)
                return tuple(out)

            most = tuple(jnp.full((queries, 128), masked_score, f32) for _ in range(kv_heads))
            most = lax.fori_loop(0, blocks, score, most)
            tops = []
            sums = []
            totals = []
            for j in range(kv_heads):
                s = lax.dot_general(
                    qs[j], kn_scr[r, j].astype(bf16), nt, preferred_element_type=f32
                )
                s = jnp.where(allowed, s, masked_score)
                top = jnp.maximum(
                    jnp.max(most[j], axis=1, keepdims=True), jnp.max(s, axis=1, keepdims=True)
                )
                p = jnp.exp2((s - top) * factor)
                tops.append(top)
                sums.append(jnp.sum(p, axis=1, keepdims=True))
                totals.append(
                    jnp.dot(p.astype(bf16), vn_scr[r, j].astype(bf16), preferred_element_type=f32)
                )

            def gather(i, carry):
                start = pl.multiple_of(i * block, block)
                lanes, accs = carry
                new_lanes = []
                new_accs = []
                for j in range(kv_heads):
                    p = jnp.exp2((s_scr[j, :, pl.ds(start, block)] - tops[j]) * factor)
                    lane = lanes[j]
                    for b in range(block // 128):
                        lane = lane + p[:, b * 128 : (b + 1) * 128]
                    new_lanes.append(lane)
                    new_accs.append(
                        accs[j]
                        + jnp.dot(
                            p.astype(bf16),
                            v_ref[r, j, pl.ds(start, block), :],
                            preferred_element_type=f32,
                        )
                    )
                return tuple(new_lanes), tuple(new_accs)

            lanes = tuple(jnp.zeros((queries, 128), f32) for _ in range(kv_heads))
            lanes, accs = lax.fori_loop(0, blocks, gather, (lanes, tuple(totals)))
            for j in range(kv_heads):
                total_sum = sums[j] + jnp.sum(lanes[j], axis=1, keepdims=True)
                o = (accs[j] / total_sum).astype(bf16)
                for g in range(group):
                    col = (j * group + g) * head_dim
                    for n in range(copies):
                        out_ref[n, r * steps : (r + 1) * steps, col : col + head_dim] = o[
                            g * steps : (g + 1) * steps
                        ]

    flops = 4 * row_count * kv_heads * queries * cache_len * head_dim
    return pl.pallas_call(
        kernel,
        out_shape=jax.ShapeDtypeStruct((copies, lines, q_width), bf16),
        in_specs=[scalars] + [whole] * 7,
        out_specs=whole,
        scratch_shapes=[
            pltpu.VMEM((row_count, kv_heads, queries, head_dim), f32),
            pltpu.VMEM((row_count, kv_heads, fresh, head_dim), f32),
            pltpu.VMEM((row_count, kv_heads, fresh, head_dim), f32),
            pltpu.VMEM((kv_heads, queries, cache_len), f32),
        ],
        compiler_params=params(16),
        cost_estimate=pl.CostEstimate(
            flops=flops,
            bytes_accessed=4 * row_count * kv_heads * cache_len * head_dim,
            transcendentals=0,
        ),
        name="attention",
    )(live, parts, scale, bias, cosine, sine, in_vmem(key_cache), in_vmem(value_cache))


def project(core, gathered, weights):
    sources, per, width = gathered.shape
    tp = lax.axis_size("tp")
    chips = sources // tp
    cores = len(weights)
    columns = weights[0].shape[1]

    def kernel(core_ref, a_ref, *refs):
        out_ref = refs[-1]
        first = core_ref[0] == 0
        accs = [None] * cores
        for t in range(tp):
            lhs = jnp.concatenate([a_ref[n * tp + t] for n in range(chips)], axis=0)
            for c in range(cores):
                part = jnp.dot(
                    lhs, refs[c][t * width : (t + 1) * width, :], preferred_element_type=f32
                )
                accs[c] = part if accs[c] is None else accs[c] + part
        if cores == 2:
            accs = [jnp.where(first, accs[0], accs[1]), jnp.where(first, accs[1], accs[0])]
        acc = jnp.concatenate(accs, axis=1).astype(bf16)
        for n in range(chips):
            for t in range(tp):
                out_ref[n * tp + t] = acc[n * per : (n + 1) * per]

    return pl.pallas_call(
        kernel,
        out_shape=jax.ShapeDtypeStruct((sources, per, cores * columns), bf16),
        in_specs=[scalars] + [whole] * (1 + cores),
        out_specs=whole,
        compiler_params=params(16),
        cost_estimate=pl.CostEstimate(
            flops=2 * chips * per * tp * width * cores * columns,
            bytes_accessed=2 * tp * width * cores * columns,
            transcendentals=0,
        ),
        name="project",
    )(core, gathered, *weights)


def shards(
    hidden_in,
    norm_gain,
    w_query,
    key_weight_matrix,
    value_weight_matrix,
    bias_query,
    key_bias_vector,
    value_bias_vector,
    w_out,
    key_cache,
    value_cache,
    lengths,
    finished,
):
    step_count, row_count, model_width = hidden_in.shape
    lines = step_count * row_count
    head_dim = key_cache.shape[3]
    chips = lax.axis_size("chip")
    cores = lax.axis_size("core")
    tp = lax.axis_size("tp")
    core = lax.axis_index("core")
    tp_index = lax.axis_index("tp")
    width = model_width // (chips * cores * tp)
    plane = ("chip", "tp")
    swap = [(i, cores - 1 - i) for i in range(cores)]

    def both(weight):
        return [weight] + ([lax.ppermute(weight, "core", swap)] if cores == 2 else [])

    queries_w = both(w_query)
    keys_w = both(key_weight_matrix)
    values_w = both(value_weight_matrix)
    outs_w = both(w_out)

    by_row = jnp.transpose(hidden_in, (1, 0, 2)).reshape(lines, model_width)
    widened = by_row.astype(f32)
    gained = (widened * norm_gain.astype(f32)).astype(bf16)
    blocked = gained.reshape(lines, chips, cores, tp, width)
    mine = lax.dynamic_index_in_dim(blocked, tp_index, 3, keepdims=False)
    if cores == 2:
        mine = jnp.where(core == 0, mine, mine[:, :, ::-1])
    mine = jnp.transpose(mine, (1, 2, 0, 3)).reshape(chips, cores * lines, width)
    columns = lax.all_to_all(mine, "chip", split_axis=0, concat_axis=0, tiled=True)
    columns = columns.reshape(chips, cores, lines, width)
    columns = jnp.transpose(columns, (1, 0, 2, 3)).reshape(cores, chips * lines, width)
    weights = list(zip(queries_w, keys_w, values_w))
    partials = qkv_partials(columns, weights)
    parts = lax.all_to_all(partials, plane, split_axis=0, concat_axis=0, tiled=True)

    scale = lax.rsqrt(jnp.mean(widened * widened, axis=-1, keepdims=True) + norm_eps)
    scale = jnp.broadcast_to(scale, (lines, head_dim))
    bias = jnp.concatenate([bias_query, key_bias_vector, value_bias_vector])[None]
    position = (lengths[:, None] + jnp.arange(step_count, dtype=jnp.int32)[None]).astype(f32)
    half = head_dim // 2
    lane = jnp.arange(head_dim)
    pair = (lane % half).astype(f32)
    frequency = jnp.exp(pair * (-2.0 * math.log(rope_base) / head_dim))
    angles = position.reshape(lines, 1) * frequency
    cosine = jnp.cos(angles)
    sine = jnp.where(lane < half, -1.0, 1.0) * jnp.sin(angles)
    live = jnp.where(finished != 0, 0, lengths)
    attended = attention(
        live, parts, scale, bias, cosine, sine, key_cache, value_cache, chips * tp
    )
    gathered = lax.all_to_all(attended, plane, split_axis=0, concat_axis=0, tiled=True)
    product = project(core.astype(jnp.int32).reshape(1), gathered, outs_w)
    arrived = lax.all_to_all(product, plane, split_axis=0, concat_axis=0, tiled=True)
    arrived = arrived.reshape(chips, tp, row_count, step_count, cores, width)
    projected = jnp.transpose(arrived, (3, 2, 0, 4, 1, 5)).reshape(
        step_count, row_count, model_width
    )
    hidden = hidden_in.astype(f32)
    layer_out = jnp.where(finished[None, :, None] != 0, hidden, hidden + projected.astype(f32))
    return layer_out.astype(bf16)


def solution(mesh):
    gen = mesh.shape["gen"]
    cores = 2 if gen % 2 == 0 else 1
    split = Mesh(
        mesh.devices.reshape(gen // cores, cores, mesh.shape["tp"]), ("chip", "core", "tp")
    )
    rows = ("chip", "core")
    every = ("chip", "core", "tp")
    placed = (
        P(None, rows, None),
        P(),
        P(every, None),
        P(every, None),
        P(every, None),
        P("tp"),
        P("tp"),
        P("tp"),
        P(None, every),
        P(rows, "tp", None, None),
        P(rows, "tp", None, None),
        P(rows),
        P(rows),
    )
    return jax.shard_map(
        shards, mesh=split, in_specs=placed, out_specs=P(None, rows, None), check_vma=False
    )
```

```python
import math

import jax
import jax.numpy as jnp
from jax import lax
from jax.experimental import pallas as pl
from jax.experimental.pallas import tpu as pltpu
from jax.sharding import Mesh
from jax.sharding import PartitionSpec as P

norm_eps = 1e-06
rope_base = 1000000.0
masked_score = -1e30
bf16 = jnp.bfloat16
f32 = jnp.float32


whole = pl.BlockSpec(memory_space=pltpu.VMEM)
scalars = pl.BlockSpec(memory_space=pltpu.SMEM)
distant = pl.BlockSpec(memory_space=pltpu.HBM)


def far_away(array):
    return pltpu.with_memory_space_constraint(array, pltpu.HBM)


def params(mib):
    return pltpu.CompilerParams(vmem_limit_bytes=mib << 20)


def prepare(core, tp_index, hidden_in, norm_gain, chips, cores, tp):
    step_count, row_count, model_width = hidden_in.shape
    lines = step_count * row_count
    width = model_width // (chips * cores * tp)

    def kernel(core_ref, tp_ref, h_hbm, g_hbm, mine_ref, scale_ref, h_ref, g_ref, x_scr, g_scr, sems):
        copies = [
            pltpu.make_async_copy(h_hbm, h_ref, sems.at[0]),
            pltpu.make_async_copy(g_hbm, g_ref, sems.at[1]),
        ]
        for copy in copies:
            copy.start()
        for copy in copies:
            copy.wait()
        for s in range(step_count):
            x = h_ref[s].astype(f32)
            for r in range(row_count):
                x_scr[r * step_count + s : r * step_count + s + 1, :] = x[r : r + 1]
        g_scr[...] = g_ref[...].astype(f32)
        own = core_ref[0]
        for n in range(chips):
            for c in range(cores):
                at = own if c == 0 else 1 - own
                block = ((n * cores + at) * tp + tp_ref[0]) * (width // 128)
                for b in range(width // 128):
                    start = pl.multiple_of((block + b) * 128, 128)
                    x = x_scr[:, pl.ds(start, 128)] * g_scr[pl.ds(block + b, 1), :]
                    mine_ref[n, c * lines : (c + 1) * lines, b * 128 : (b + 1) * 128] = x.astype(
                        bf16
                    )
        square = jnp.zeros((lines, 128), f32)
        for b in range(model_width // 128):
            x = x_scr[:, b * 128 : (b + 1) * 128]
            square = square + x * x
        mean = jnp.sum(square, axis=1, keepdims=True) * (1.0 / model_width)
        scale_ref[...] = jnp.broadcast_to(lax.rsqrt(mean + norm_eps), (lines, 128))

    return pl.pallas_call(
        kernel,
        out_shape=(
            jax.ShapeDtypeStruct((chips, cores * lines, width), bf16),
            jax.ShapeDtypeStruct((lines, 128), f32),
        ),
        in_specs=[scalars, scalars, distant, distant],
        out_specs=(whole, whole),
        scratch_shapes=[
            pltpu.VMEM(hidden_in.shape, bf16),
            pltpu.VMEM((model_width // 128, 128), bf16),
            pltpu.VMEM((lines, model_width), f32),
            pltpu.VMEM((model_width // 128, 128), f32),
            pltpu.SemaphoreType.DMA((2,)),
        ],
        compiler_params=params(4),
        name="prepare",
    )(
        core,
        tp_index,
        far_away(hidden_in),
        far_away(norm_gain.reshape(model_width // 128, 128)),
    )


def qkv_partials(columns, weights):
    chips, depth, width = columns.shape
    cores = len(weights)
    tp = lax.axis_size("tp")
    per = depth // cores
    rows = chips * per
    sizes = [w.shape[1] // tp for w in weights[0]]
    total = sum(sizes)
    near = weights[-1]
    fetched = [w for group in weights[:-1] for w in group]

    def kernel(x_ref, *refs):
        near_refs, sources, out_ref = refs[:3], refs[3 : 3 + len(fetched)], refs[3 + len(fetched)]
        held, acc_scr, sems = refs[4 + len(fetched) : -2], refs[-2], refs[-1]
        pieces = [
            (c, 0, pl.ds(t * sizes[0], sizes[0])) for c in range(cores - 1) for t in range(tp)
        ] + [(c, kind, pl.ds(0, tp * sizes[kind])) for c in range(cores - 1) for kind in (1, 2)]
        copies = {}
        for k, (c, kind, part) in enumerate(pieces):
            copies[k] = pltpu.make_async_copy(
                sources[3 * c + kind].at[:, part], held[3 * c + kind].at[:, part], sems.at[k]
            )
            copies[k].start()
        lhs = [
            jnp.concatenate([x_ref[n, c * per : (c + 1) * per] for n in range(chips)], axis=0)
            for c in range(cores)
        ]

        def put(t, kind, value):
            value = value.astype(bf16)
            start = sum(sizes[:kind])
            for n in range(chips):
                out_ref[n * tp + t, :, start : start + sizes[kind]] = value[
                    n * per : (n + 1) * per
                ]

        def times(c, ref, t, kind):
            piece = ref[:, t * sizes[kind] : (t + 1) * sizes[kind]]
            return jnp.dot(lhs[c], piece, preferred_element_type=f32)

        for t in range(tp):
            for kind in range(3):
                start = sum(sizes[:kind])
                acc = times(cores - 1, near_refs[kind], t, kind)
                if cores == 1:
                    put(t, kind, acc)
                else:
                    acc_scr[t, :, start : start + sizes[kind]] = acc
        for k, (c, kind, part) in enumerate(pieces):
            copies[k].wait()
            start = sum(sizes[:kind])
            for t in [k % tp] if kind == 0 else range(tp):
                acc = acc_scr[t, :, start : start + sizes[kind]]
                put(t, kind, acc + times(c, held[3 * c + kind], t, kind))

    flops = 2 * cores * rows * width * total * tp
    return pl.pallas_call(
        kernel,
        out_shape=jax.ShapeDtypeStruct((chips * tp, per, total), bf16),
        in_specs=[whole] * 4 + [distant] * len(fetched),
        out_specs=whole,
        scratch_shapes=[pltpu.VMEM(w.shape, w.dtype) for w in fetched]
        + [
            pltpu.VMEM((tp, rows, total), f32),
            pltpu.SemaphoreType.DMA((max(1, (cores - 1) * (tp + 2)),)),
        ],
        compiler_params=params(16),
        cost_estimate=pl.CostEstimate(
            flops=flops, bytes_accessed=2 * cores * width * total * tp, transcendentals=0
        ),
        name="qkv_partials",
    )(columns, *near, *[far_away(w) for w in fetched])


def attention(lengths, finished, parts, scale, biases, key_cache, value_cache, copies, block):
    sources, lines, total = parts.shape
    row_count, kv_heads, cache_len, head_dim = key_cache.shape
    steps = lines // row_count
    kv_width = kv_heads * head_dim
    q_width = total - 2 * kv_width
    heads = q_width // head_dim
    group = heads // kv_heads
    queries = group * steps
    fresh = 8
    factor = math.log2(math.e) / math.sqrt(head_dim)

    def kernel(length_ref, finished_ref, p_ref, scale_ref, bq_ref, bk_ref, bv_ref, k_ref, v_ref,
               out_ref, k_scr, v_scr, q_scr, kn_scr, vn_scr, s_scr, sems):
        lives = [
            jnp.where(finished_ref[r] != 0, 0, length_ref[r]) for r in range(row_count)
        ]
        counts = [(length + block - 1) // block for length in lives]

        def fetch(r, kind, i, act):
            source, target = ((k_ref, k_scr), (v_ref, v_scr))[kind]
            part = pl.ds(pl.multiple_of(i * block, block), block)
            act(
                pltpu.make_async_copy(
                    source.at[r, :, part, :], target.at[r, :, part, :], sems.at[r, kind, i]
                )
            )

        for r in range(row_count):
            for kind in range(2):
                def start_one(i, carry):
                    fetch(r, kind, i, lambda copy: copy.start())
                    return carry

                lax.fori_loop(0, counts[r], start_one, 0)
        scale = scale_ref[...]
        line = lax.broadcasted_iota(jnp.int32, (lines, head_dim), 0)
        lane = lax.broadcasted_iota(jnp.int32, (lines, head_dim), 1)
        position = line % steps
        for r in range(row_count):
            position = position + jnp.where(line // steps == r, length_ref[r], 0)
        half = head_dim // 2
        pair = (lane % half).astype(f32)
        frequency = jnp.exp(pair * (-2.0 * math.log(rope_base) / head_dim))
        angles = position.astype(f32) * frequency
        cos = jnp.cos(angles)
        sin = jnp.where(lane < half, -1.0, 1.0) * jnp.sin(angles)

        def summed(start, bias_row):
            part = p_ref[0, :, start : start + head_dim].astype(f32)
            for i in range(1, sources):
                part = part + p_ref[i, :, start : start + head_dim].astype(f32)
            return part * scale + bias_row.astype(f32)

        def rotated(start, bias_row):
            head = summed(start, bias_row)
            return head * cos + pltpu.roll(head, half, 1) * sin

        kn_scr[...] = jnp.zeros_like(kn_scr)
        vn_scr[...] = jnp.zeros_like(vn_scr)
        for h in range(heads):
            q = rotated(h * head_dim, bq_ref[h : h + 1, :])
            for r in range(row_count):
                g = h % group
                q_scr[r, h // group, g * steps : (g + 1) * steps, :] = q[r * steps : (r + 1) * steps]
        for j in range(kv_heads):
            k = rotated(q_width + j * head_dim, bk_ref[j : j + 1, :])
            v = summed(q_width + kv_width + j * head_dim, bv_ref[j : j + 1, :])
            for r in range(row_count):
                kn_scr[r, j, 0:steps, :] = k[r * steps : (r + 1) * steps]
                vn_scr[r, j, 0:steps, :] = v[r * steps : (r + 1) * steps]
        step_of = lax.broadcasted_iota(jnp.int32, (queries, fresh), 0) % steps
        allowed = lax.broadcasted_iota(jnp.int32, (queries, fresh), 1) <= step_of
        nt = (((1,), (1,)), ((), ()))
        for r in range(row_count):
            length = lives[r]
            blocks = counts[r]
            qs = [q_scr[r, j].astype(bf16) for j in range(kv_heads)]

            def score(i, most):
                start = pl.multiple_of(i * block, block)
                fetch(r, 0, i, lambda copy: copy.wait())
                place = start + lax.broadcasted_iota(jnp.int32, (queries, block), 1)
                inside = place < length
                out = []
                for j in range(kv_heads):
                    s = lax.dot_general(
                        qs[j], k_scr[r, j, pl.ds(start, block), :], nt, preferred_element_type=f32
                    )
                    s = jnp.where(inside, s, masked_score)
                    s_scr[j, :, pl.ds(start, block)] = s
                    top = most[j]
                    for b in range(block // 128):
                        top = jnp.maximum(top, s[:, b * 128 : (b + 1) * 128])
                    out.append(top)
                return tuple(out)

            most = tuple(jnp.full((queries, 128), masked_score, f32) for _ in range(kv_heads))
            most = lax.fori_loop(0, blocks, score, most)
            tops = []
            sums = []
            totals = []
            for j in range(kv_heads):
                s = lax.dot_general(
                    qs[j], kn_scr[r, j].astype(bf16), nt, preferred_element_type=f32
                )
                s = jnp.where(allowed, s, masked_score)
                top = jnp.maximum(
                    jnp.max(most[j], axis=1, keepdims=True), jnp.max(s, axis=1, keepdims=True)
                )
                p = jnp.exp2((s - top) * factor)
                tops.append(top)
                sums.append(jnp.sum(p, axis=1, keepdims=True))
                totals.append(
                    jnp.dot(p.astype(bf16), vn_scr[r, j].astype(bf16), preferred_element_type=f32)
                )

            def gather(i, carry):
                start = pl.multiple_of(i * block, block)
                fetch(r, 1, i, lambda copy: copy.wait())
                lanes, accs = carry
                new_lanes = []
                new_accs = []
                for j in range(kv_heads):
                    p = jnp.exp2((s_scr[j, :, pl.ds(start, block)] - tops[j]) * factor)
                    lane = lanes[j]
                    for b in range(block // 128):
                        lane = lane + p[:, b * 128 : (b + 1) * 128]
                    new_lanes.append(lane)
                    new_accs.append(
                        accs[j]
                        + jnp.dot(
                            p.astype(bf16),
                            v_scr[r, j, pl.ds(start, block), :],
                            preferred_element_type=f32,
                        )
                    )
                return tuple(new_lanes), tuple(new_accs)

            lanes = tuple(jnp.zeros((queries, 128), f32) for _ in range(kv_heads))
            lanes, accs = lax.fori_loop(0, blocks, gather, (lanes, tuple(totals)))
            for j in range(kv_heads):
                total_sum = sums[j] + jnp.sum(lanes[j], axis=1, keepdims=True)
                o = (accs[j] / total_sum).astype(bf16)
                for g in range(group):
                    col = (j * group + g) * head_dim
                    for n in range(copies):
                        out_ref[n, r * steps : (r + 1) * steps, col : col + head_dim] = o[
                            g * steps : (g + 1) * steps
                        ]

    flops = 4 * row_count * kv_heads * queries * cache_len * head_dim
    return pl.pallas_call(
        kernel,
        out_shape=jax.ShapeDtypeStruct((copies, lines, q_width), bf16),
        in_specs=[scalars, scalars] + [whole] * 5 + [distant] * 2,
        out_specs=whole,
        scratch_shapes=[
            pltpu.VMEM(key_cache.shape, bf16),
            pltpu.VMEM(value_cache.shape, bf16),
            pltpu.VMEM((row_count, kv_heads, queries, head_dim), f32),
            pltpu.VMEM((row_count, kv_heads, fresh, head_dim), f32),
            pltpu.VMEM((row_count, kv_heads, fresh, head_dim), f32),
            pltpu.VMEM((kv_heads, queries, cache_len), f32),
            pltpu.SemaphoreType.DMA((row_count, 2, cache_len // block)),
        ],
        compiler_params=params(48),
        cost_estimate=pl.CostEstimate(
            flops=flops,
            bytes_accessed=4 * row_count * kv_heads * cache_len * head_dim,
            transcendentals=0,
        ),
        name="attention",
    )(
        lengths,
        finished,
        parts,
        scale,
        *[b.reshape(-1, head_dim) for b in biases],
        far_away(key_cache),
        far_away(value_cache),
    )


def project(core, gathered, weights):
    sources, per, width = gathered.shape
    tp = lax.axis_size("tp")
    chips = sources // tp
    cores = len(weights)
    columns = weights[0].shape[1]

    def kernel(core_ref, a_ref, near_ref, *refs):
        far = refs[: cores - 1]
        out_ref, held, sems = refs[cores - 1], refs[cores : 2 * cores - 1], refs[-1]
        first = core_ref[0] == 0
        copies = []
        for t in range(tp):
            part = pl.ds(t * width, width)
            for c in range(cores - 1):
                copies.append(
                    pltpu.make_async_copy(far[c].at[part, :], held[c].at[part, :], sems.at[t])
                )
                copies[-1].start()
        lhs = [
            jnp.concatenate([a_ref[n * tp + t] for n in range(chips)], axis=0) for t in range(tp)
        ]
        accs = []
        for c in range(cores):
            acc = None
            for t in range(tp):
                source = near_ref
                if c:
                    copies[t].wait()
                    source = held[c - 1]
                part = jnp.dot(
                    lhs[t], source[t * width : (t + 1) * width, :], preferred_element_type=f32
                )
                acc = part if acc is None else acc + part
            accs.append(acc)
        if cores == 2:
            accs = [jnp.where(first, accs[0], accs[1]), jnp.where(first, accs[1], accs[0])]
        acc = jnp.concatenate(accs, axis=1).astype(bf16)
        for n in range(chips):
            for t in range(tp):
                out_ref[n * tp + t] = acc[n * per : (n + 1) * per]

    return pl.pallas_call(
        kernel,
        out_shape=jax.ShapeDtypeStruct((sources, per, cores * columns), bf16),
        in_specs=[scalars, whole, whole] + [distant] * (cores - 1),
        out_specs=whole,
        scratch_shapes=[pltpu.VMEM(w.shape, w.dtype) for w in weights[1:]]
        + [pltpu.SemaphoreType.DMA((tp,))],
        compiler_params=params(16),
        cost_estimate=pl.CostEstimate(
            flops=2 * chips * per * tp * width * cores * columns,
            bytes_accessed=2 * tp * width * cores * columns,
            transcendentals=0,
        ),
        name="project",
    )(core, gathered, *weights)


def shards(
    hidden_in,
    norm_gain,
    w_query,
    key_weight_matrix,
    value_weight_matrix,
    bias_query,
    key_bias_vector,
    value_bias_vector,
    w_out,
    key_cache,
    value_cache,
    lengths,
    finished,
):
    step_count, row_count, model_width = hidden_in.shape
    lines = step_count * row_count
    head_dim = key_cache.shape[3]
    chips = lax.axis_size("chip")
    cores = lax.axis_size("core")
    tp = lax.axis_size("tp")
    core = lax.axis_index("core")
    tp_index = lax.axis_index("tp")
    width = model_width // (chips * cores * tp)
    plane = ("chip", "tp")
    swap = [(i, cores - 1 - i) for i in range(cores)]

    def both(weight):
        return [weight] + ([lax.ppermute(weight, "core", swap)] if cores == 2 else [])

    queries_w = both(w_query)
    keys_w = both(key_weight_matrix)
    values_w = both(value_weight_matrix)
    outs_w = both(w_out)

    core_place = core.astype(jnp.int32).reshape(1)
    tp_place = tp_index.astype(jnp.int32).reshape(1)
    if width % 128 == 0:
        mine, scale = prepare(core_place, tp_place, hidden_in, norm_gain, chips, cores, tp)
    else:
        by_row = jnp.transpose(hidden_in, (1, 0, 2)).reshape(lines, model_width).astype(f32)
        blocked = (by_row * norm_gain.astype(f32)).astype(bf16)
        blocked = blocked.reshape(lines, chips, cores, tp, width)
        mine = lax.dynamic_index_in_dim(blocked, tp_index, 3, keepdims=False)
        if cores == 2:
            mine = jnp.where(core == 0, mine, mine[:, :, ::-1])
        mine = jnp.transpose(mine, (1, 2, 0, 3)).reshape(chips, cores * lines, width)
        scale = lax.rsqrt(jnp.mean(by_row * by_row, axis=-1, keepdims=True) + norm_eps)
        scale = jnp.broadcast_to(scale, (lines, 128))
    columns = lax.all_to_all(mine, "chip", split_axis=0, concat_axis=0, tiled=True)
    partials = qkv_partials(columns, list(zip(queries_w, keys_w, values_w)))
    parts = lax.all_to_all(partials, plane, split_axis=0, concat_axis=0, tiled=True)
    block = min(key_cache.shape[2], 2048)
    attended = attention(
        lengths,
        finished,
        parts,
        scale,
        (bias_query, key_bias_vector, value_bias_vector),
        key_cache,
        value_cache,
        chips * tp,
        block,
    )
    gathered = lax.all_to_all(attended, plane, split_axis=0, concat_axis=0, tiled=True)
    product = project(core_place, gathered, outs_w)
    arrived = lax.all_to_all(product, plane, split_axis=0, concat_axis=0, tiled=True)
    arrived = arrived.reshape(chips, tp, row_count, step_count, cores, width)
    projected = jnp.transpose(arrived, (3, 2, 0, 4, 1, 5)).reshape(
        step_count, row_count, model_width
    )
    hidden = hidden_in.astype(f32)
    layer_out = jnp.where(finished[None, :, None] != 0, hidden, hidden + projected.astype(f32))
    return layer_out.astype(bf16)


def solution(mesh):
    gen = mesh.shape["gen"]
    cores = 2 if gen % 2 == 0 else 1
    split = Mesh(
        mesh.devices.reshape(gen // cores, cores, mesh.shape["tp"]), ("chip", "core", "tp")
    )
    rows = ("chip", "core")
    every = ("chip", "core", "tp")
    placed = (
        P(None, rows, None),
        P(),
        P(every, None),
        P(every, None),
        P(every, None),
        P("tp"),
        P("tp"),
        P("tp"),
        P(None, every),
        P(rows, "tp", None, None),
        P(rows, "tp", None, None),
        P(rows),
        P(rows),
    )
    return jax.shard_map(
        shards, mesh=split, in_specs=placed, out_specs=P(None, rows, None), check_vma=False
    )
```

```python
import math

import jax
import jax.numpy as jnp
from jax import lax
from jax.experimental import pallas as pl
from jax.experimental.pallas import tpu as pltpu
from jax.sharding import Mesh
from jax.sharding import PartitionSpec as P

norm_eps = 1e-06
rope_base = 1000000.0
masked_score = -1e30
bf16 = jnp.bfloat16
f32 = jnp.float32


whole = pl.BlockSpec(memory_space=pltpu.VMEM)
scalars = pl.BlockSpec(memory_space=pltpu.SMEM)
distant = pl.BlockSpec(memory_space=pltpu.HBM)


def far_away(array):
    return pltpu.with_memory_space_constraint(array, pltpu.HBM)


def params(mib):
    return pltpu.CompilerParams(vmem_limit_bytes=mib << 20)


def prepare(core, tp_index, hidden_in, norm_gain, chips, cores, tp):
    step_count, row_count, model_width = hidden_in.shape
    lines = step_count * row_count
    width = model_width // (chips * cores * tp)

    def kernel(core_ref, tp_ref, h_hbm, g_hbm, mine_ref, scale_ref, h_ref, g_ref, x_scr, g_scr, sems):
        copies = [
            pltpu.make_async_copy(h_hbm, h_ref, sems.at[0]),
            pltpu.make_async_copy(g_hbm, g_ref, sems.at[1]),
        ]
        for copy in copies:
            copy.start()
        for copy in copies:
            copy.wait()
        for s in range(step_count):
            x = h_ref[s].astype(f32)
            for r in range(row_count):
                x_scr[r * step_count + s : r * step_count + s + 1, :] = x[r : r + 1]
        g_scr[...] = g_ref[...].astype(f32)
        own = core_ref[0]
        for n in range(chips):
            for c in range(cores):
                at = own if c == 0 else 1 - own
                block = ((n * cores + at) * tp + tp_ref[0]) * (width // 128)
                for b in range(width // 128):
                    start = pl.multiple_of((block + b) * 128, 128)
                    x = x_scr[:, pl.ds(start, 128)] * g_scr[pl.ds(block + b, 1), :]
                    mine_ref[n, c * lines : (c + 1) * lines, b * 128 : (b + 1) * 128] = x.astype(
                        bf16
                    )
        square = jnp.zeros((lines, 128), f32)
        for b in range(model_width // 128):
            x = x_scr[:, b * 128 : (b + 1) * 128]
            square = square + x * x
        mean = jnp.sum(square, axis=1, keepdims=True) * (1.0 / model_width)
        scale_ref[...] = jnp.broadcast_to(lax.rsqrt(mean + norm_eps), (lines, 128))

    return pl.pallas_call(
        kernel,
        out_shape=(
            jax.ShapeDtypeStruct((chips, cores * lines, width), bf16),
            jax.ShapeDtypeStruct((lines, 128), f32),
        ),
        in_specs=[scalars, scalars, distant, distant],
        out_specs=(whole, whole),
        scratch_shapes=[
            pltpu.VMEM(hidden_in.shape, bf16),
            pltpu.VMEM((model_width // 128, 128), bf16),
            pltpu.VMEM((lines, model_width), f32),
            pltpu.VMEM((model_width // 128, 128), f32),
            pltpu.SemaphoreType.DMA((2,)),
        ],
        compiler_params=params(4),
        name="prepare",
    )(
        core,
        tp_index,
        far_away(hidden_in),
        far_away(norm_gain.reshape(model_width // 128, 128)),
    )


def qkv_partials(columns, weights):
    chips, depth, width = columns.shape
    cores = len(weights)
    tp = lax.axis_size("tp")
    per = depth // cores
    rows = chips * per
    sizes = [w.shape[1] // tp for w in weights[0]]
    total = sum(sizes)
    near = weights[-1]
    fetched = [w for group in weights[:-1] for w in group]

    def kernel(x_ref, *refs):
        near_refs, sources, out_ref = refs[:3], refs[3 : 3 + len(fetched)], refs[3 + len(fetched)]
        held, acc_scr, sems = refs[4 + len(fetched) : -2], refs[-2], refs[-1]
        pieces = [
            (c, 0, pl.ds(t * sizes[0], sizes[0])) for c in range(cores - 1) for t in range(tp)
        ] + [(c, kind, pl.ds(0, tp * sizes[kind])) for c in range(cores - 1) for kind in (1, 2)]
        copies = {}
        for k, (c, kind, part) in enumerate(pieces):
            copies[k] = pltpu.make_async_copy(
                sources[3 * c + kind].at[:, part], held[3 * c + kind].at[:, part], sems.at[k]
            )
            copies[k].start()
        lhs = [
            jnp.concatenate([x_ref[n, c * per : (c + 1) * per] for n in range(chips)], axis=0)
            for c in range(cores)
        ]

        def put(t, kind, value):
            value = value.astype(bf16)
            start = sum(sizes[:kind])
            for n in range(chips):
                out_ref[n * tp + t, :, start : start + sizes[kind]] = value[
                    n * per : (n + 1) * per
                ]

        def times(c, ref, t, kind):
            piece = ref[:, t * sizes[kind] : (t + 1) * sizes[kind]]
            return jnp.dot(lhs[c], piece, preferred_element_type=f32)

        for t in range(tp):
            for kind in range(3):
                start = sum(sizes[:kind])
                acc = times(cores - 1, near_refs[kind], t, kind)
                if cores == 1:
                    put(t, kind, acc)
                else:
                    acc_scr[t, :, start : start + sizes[kind]] = acc
        for k, (c, kind, part) in enumerate(pieces):
            copies[k].wait()
            start = sum(sizes[:kind])
            for t in [k % tp] if kind == 0 else range(tp):
                acc = acc_scr[t, :, start : start + sizes[kind]]
                put(t, kind, acc + times(c, held[3 * c + kind], t, kind))

    flops = 2 * cores * rows * width * total * tp
    return pl.pallas_call(
        kernel,
        out_shape=pltpu.VMEM((chips * tp, per, total), bf16),
        in_specs=[whole] * 4 + [distant] * len(fetched),
        out_specs=whole,
        scratch_shapes=[pltpu.VMEM(w.shape, w.dtype) for w in fetched]
        + [
            pltpu.VMEM((tp, rows, total), f32),
            pltpu.SemaphoreType.DMA((max(1, (cores - 1) * (tp + 2)),)),
        ],
        compiler_params=params(16),
        cost_estimate=pl.CostEstimate(
            flops=flops, bytes_accessed=2 * cores * width * total * tp, transcendentals=0
        ),
        name="qkv_partials",
    )(columns, *near, *[far_away(w) for w in fetched])


def attention(lengths, finished, parts, scale, biases, key_cache, value_cache, copies, block):
    sources, lines, total = parts.shape
    row_count, kv_heads, cache_len, head_dim = key_cache.shape
    steps = lines // row_count
    kv_width = kv_heads * head_dim
    q_width = total - 2 * kv_width
    heads = q_width // head_dim
    group = heads // kv_heads
    queries = group * steps
    fresh = 8
    small = min(block, 1024)
    factor = math.log2(math.e) / math.sqrt(head_dim)
    pairs = [(r, j) for r in range(row_count) for j in range(kv_heads)]

    def kernel(length_ref, finished_ref, p_ref, scale_ref, bq_ref, bk_ref, bv_ref, k_ref, v_ref,
               out_ref, k_scr, v_scr, q_scr, kn_scr, vn_scr, s_scr, o_scr, sems):
        lives = [
            jnp.where(finished_ref[r] != 0, 0, length_ref[r]) for r in range(row_count)
        ]
        larges = [length // block for length in lives]
        smalls = [
            (length - large * block + small - 1) // small for length, large in zip(lives, larges)
        ]
        tails = [large * block for large in larges]

        def fetch(r, kind, sem, start, size):
            source, target = ((k_ref, k_scr), (v_ref, v_scr))[kind]
            part = pl.ds(start, size)
            return pltpu.make_async_copy(
                source.at[r, :, part, :], target.at[r, :, part, :], sems.at[r, kind, sem]
            )

        def large_at(r, i):
            return pl.multiple_of(i * block, block)

        def small_at(r, i):
            return pl.multiple_of(tails[r] + i * small, small)

        most_large = cache_len // block

        for r in range(row_count):
            for kind in range(2):
                def start_large(i, carry):
                    fetch(r, kind, i, large_at(r, i), block).start()
                    return carry

                def start_small(i, carry):
                    fetch(r, kind, most_large + i, small_at(r, i), small).start()
                    return carry

                lax.fori_loop(0, larges[r], start_large, 0)
                lax.fori_loop(0, smalls[r], start_small, 0)
        scale = scale_ref[...]
        line = lax.broadcasted_iota(jnp.int32, (lines, head_dim), 0)
        lane = lax.broadcasted_iota(jnp.int32, (lines, head_dim), 1)
        position = line % steps
        for r in range(row_count):
            position = position + jnp.where(line // steps == r, length_ref[r], 0)
        half = head_dim // 2
        pair = (lane % half).astype(f32)
        frequency = jnp.exp(pair * (-2.0 * math.log(rope_base) / head_dim))
        angles = position.astype(f32) * frequency
        cos = jnp.cos(angles)
        sin = jnp.where(lane < half, -1.0, 1.0) * jnp.sin(angles)

        def summed(start, bias_row):
            terms = [p_ref[i, :, start : start + head_dim].astype(f32) for i in range(sources)]
            while len(terms) > 1:
                terms = [sum(terms[i : i + 2]) for i in range(0, len(terms), 2)]
            return terms[0] * scale + bias_row.astype(f32)

        def rotated(start, bias_row):
            head = summed(start, bias_row)
            return head * cos + pltpu.roll(head, half, 1) * sin

        kn_scr[...] = jnp.zeros_like(kn_scr)
        vn_scr[...] = jnp.zeros_like(vn_scr)
        for h in range(heads):
            q = rotated(h * head_dim, bq_ref[h : h + 1, :])
            for r in range(row_count):
                g = h % group
                q_scr[r, h // group, g * steps : (g + 1) * steps, :] = q[r * steps : (r + 1) * steps]
        for j in range(kv_heads):
            k = rotated(q_width + j * head_dim, bk_ref[j : j + 1, :])
            v = summed(q_width + kv_width + j * head_dim, bv_ref[j : j + 1, :])
            for r in range(row_count):
                kn_scr[r, j, 0:steps, :] = k[r * steps : (r + 1) * steps]
                vn_scr[r, j, 0:steps, :] = v[r * steps : (r + 1) * steps]
        step_of = lax.broadcasted_iota(jnp.int32, (queries, fresh), 0) % steps
        allowed = lax.broadcasted_iota(jnp.int32, (queries, fresh), 1) <= step_of
        nt = (((1,), (1,)), ((), ()))
        qs = {}
        new_scores = {}
        new_tops = {}
        for r, j in pairs:
            qs[r, j] = q_scr[r, j].astype(bf16)
            s = lax.dot_general(
                qs[r, j], kn_scr[r, j].astype(bf16), nt, preferred_element_type=f32
            )
            new_scores[r, j] = jnp.where(allowed, s, masked_score)
            new_tops[r, j] = jnp.max(new_scores[r, j], axis=1, keepdims=True)
        tops = {}
        lane_sums = {}
        totals = {}
        for r in range(row_count):

            def scores(start, size, masked, most):
                out = []
                for j in range(kv_heads):
                    s = lax.dot_general(
                        qs[r, j], k_scr[r, j, pl.ds(start, size), :], nt, preferred_element_type=f32
                    )
                    if masked:
                        place = start + lax.broadcasted_iota(jnp.int32, (queries, size), 1)
                        s = jnp.where(place < lives[r], s, masked_score)
                    s_scr[j, :, pl.ds(start, size)] = s
                    top = most[j]
                    for b in range(size // 128):
                        top = jnp.maximum(top, s[:, b * 128 : (b + 1) * 128])
                    out.append(top)
                return tuple(out)

            def score_large(i, most):
                start = large_at(r, i)
                fetch(r, 0, i, start, block).wait()
                return scores(start, block, False, most)

            def score_small(i, most):
                start = small_at(r, i)
                fetch(r, 0, most_large + i, start, small).wait()
                return scores(start, small, True, most)

            most = tuple(jnp.full((queries, 128), masked_score, f32) for _ in range(kv_heads))
            most = lax.fori_loop(0, larges[r], score_large, most)
            most = lax.fori_loop(0, smalls[r], score_small, most)
            for j in range(kv_heads):
                tops[r, j] = jnp.maximum(
                    jnp.max(most[j], axis=1, keepdims=True), new_tops[r, j]
                )

            def gather(start, size, carry):
                lanes, accs = carry
                new_lanes = []
                new_accs = []
                for j in range(kv_heads):
                    p = jnp.exp2((s_scr[j, :, pl.ds(start, size)] - tops[r, j]) * factor)
                    lane_sum = lanes[j]
                    for b in range(size // 128):
                        lane_sum = lane_sum + p[:, b * 128 : (b + 1) * 128]
                    new_lanes.append(lane_sum)
                    new_accs.append(
                        accs[j]
                        + jnp.dot(
                            p.astype(bf16),
                            v_scr[r, j, pl.ds(start, size), :],
                            preferred_element_type=f32,
                        )
                    )
                return tuple(new_lanes), tuple(new_accs)

            def gather_large(i, carry):
                start = large_at(r, i)
                fetch(r, 1, i, start, block).wait()
                return gather(start, block, carry)

            def gather_small(i, carry):
                start = small_at(r, i)
                fetch(r, 1, most_large + i, start, small).wait()
                return gather(start, small, carry)

            carry = (
                tuple(jnp.zeros((queries, 128), f32) for _ in range(kv_heads)),
                tuple(jnp.zeros((queries, head_dim), f32) for _ in range(kv_heads)),
            )
            carry = lax.fori_loop(0, larges[r], gather_large, carry)
            carry = lax.fori_loop(0, smalls[r], gather_small, carry)
            for j in range(kv_heads):
                lane_sums[r, j] = carry[0][j]
                totals[r, j] = carry[1][j]
        for r, j in pairs:
            p = jnp.exp2((new_scores[r, j] - tops[r, j]) * factor)
            total_sum = jnp.sum(lane_sums[r, j], axis=1, keepdims=True) + jnp.sum(
                p, axis=1, keepdims=True
            )
            o = totals[r, j] + jnp.dot(
                p.astype(bf16), vn_scr[r, j].astype(bf16), preferred_element_type=f32
            )
            o = o / total_sum
            for g in range(group):
                col = (j * group + g) * head_dim
                o_scr[r * steps : (r + 1) * steps, col : col + head_dim] = o[
                    g * steps : (g + 1) * steps
                ]
        result = o_scr[...].astype(bf16)
        for n in range(copies):
            out_ref[n] = result

    flops = 4 * row_count * kv_heads * queries * cache_len * head_dim
    return pl.pallas_call(
        kernel,
        out_shape=pltpu.VMEM((copies, lines, q_width), bf16),
        in_specs=[scalars, scalars] + [whole] * 5 + [distant] * 2,
        out_specs=whole,
        scratch_shapes=[
            pltpu.VMEM(key_cache.shape, bf16),
            pltpu.VMEM(value_cache.shape, bf16),
            pltpu.VMEM((row_count, kv_heads, queries, head_dim), f32),
            pltpu.VMEM((row_count, kv_heads, fresh, head_dim), f32),
            pltpu.VMEM((row_count, kv_heads, fresh, head_dim), f32),
            pltpu.VMEM((kv_heads, queries, cache_len), f32),
            pltpu.VMEM((lines, q_width), f32),
            pltpu.SemaphoreType.DMA((row_count, 2, cache_len // block + block // small)),
        ],
        compiler_params=params(48),
        cost_estimate=pl.CostEstimate(
            flops=flops,
            bytes_accessed=4 * row_count * kv_heads * cache_len * head_dim,
            transcendentals=0,
        ),
        name="attention",
    )(
        lengths,
        finished,
        parts,
        scale,
        *[b.reshape(-1, head_dim) for b in biases],
        far_away(key_cache),
        far_away(value_cache),
    )


def project(core, gathered, weights):
    sources, per, width = gathered.shape
    tp = lax.axis_size("tp")
    chips = sources // tp
    cores = len(weights)
    columns = weights[0].shape[1]

    def kernel(core_ref, a_ref, near_ref, *refs):
        far = refs[: cores - 1]
        out_ref, held, sems = refs[cores - 1], refs[cores : 2 * cores - 1], refs[-1]
        first = core_ref[0] == 0
        copies = []
        for t in range(tp):
            part = pl.ds(t * width, width)
            for c in range(cores - 1):
                copies.append(
                    pltpu.make_async_copy(far[c].at[part, :], held[c].at[part, :], sems.at[t])
                )
                copies[-1].start()
        lhs = [
            jnp.concatenate([a_ref[n * tp + t] for n in range(chips)], axis=0) for t in range(tp)
        ]
        accs = []
        for c in range(cores):
            acc = None
            for t in range(tp):
                source = near_ref
                if c:
                    copies[t].wait()
                    source = held[c - 1]
                part = jnp.dot(
                    lhs[t], source[t * width : (t + 1) * width, :], preferred_element_type=f32
                )
                acc = part if acc is None else acc + part
            accs.append(acc)
        if cores == 2:
            accs = [jnp.where(first, accs[0], accs[1]), jnp.where(first, accs[1], accs[0])]
        acc = jnp.concatenate(accs, axis=1).astype(bf16)
        for n in range(chips):
            for t in range(tp):
                out_ref[n * tp + t] = acc[n * per : (n + 1) * per]

    return pl.pallas_call(
        kernel,
        out_shape=pltpu.VMEM((sources, per, cores * columns), bf16),
        in_specs=[scalars, whole, whole] + [distant] * (cores - 1),
        out_specs=whole,
        scratch_shapes=[pltpu.VMEM(w.shape, w.dtype) for w in weights[1:]]
        + [pltpu.SemaphoreType.DMA((tp,))],
        compiler_params=params(16),
        cost_estimate=pl.CostEstimate(
            flops=2 * chips * per * tp * width * cores * columns,
            bytes_accessed=2 * tp * width * cores * columns,
            transcendentals=0,
        ),
        name="project",
    )(core, gathered, *weights)


def finish(finished, arrived, hidden_in, cores):
    sources, lines, wide = arrived.shape
    step_count, row_count, model_width = hidden_in.shape
    tp = lax.axis_size("tp")
    width = wide // cores

    def kernel(finished_ref, a_ref, h_ref, out_ref, y_scr):
        for i in range(sources):
            n, t = divmod(i, tp)
            for c in range(cores):
                start = ((n * cores + c) * tp + t) * width
                y_scr[:, start : start + width] = a_ref[i, :, c * width : (c + 1) * width].astype(
                    f32
                )
        row = lax.broadcasted_iota(jnp.int32, (row_count, 1), 0)
        done = jnp.zeros((row_count, 1), jnp.int32)
        for r in range(row_count):
            done = jnp.where(row == r, finished_ref[r], done)
        for s in range(step_count):
            hidden = h_ref[s].astype(f32)
            lines_of = [r * step_count + s for r in range(row_count)]
            moved = hidden + jnp.concatenate([y_scr[i : i + 1, :] for i in lines_of], axis=0)
            out_ref[s] = jnp.where(done != 0, hidden, moved).astype(bf16)

    return pl.pallas_call(
        kernel,
        out_shape=jax.ShapeDtypeStruct(hidden_in.shape, bf16),
        in_specs=[scalars, whole, whole],
        out_specs=whole,
        scratch_shapes=[pltpu.VMEM((lines, model_width), f32)],
        compiler_params=params(4),
        name="finish",
    )(finished, arrived, hidden_in)


def shards(
    hidden_in,
    norm_gain,
    w_query,
    key_weight_matrix,
    value_weight_matrix,
    bias_query,
    key_bias_vector,
    value_bias_vector,
    w_out,
    key_cache,
    value_cache,
    lengths,
    finished,
):
    step_count, row_count, model_width = hidden_in.shape
    lines = step_count * row_count
    head_dim = key_cache.shape[3]
    chips = lax.axis_size("chip")
    cores = lax.axis_size("core")
    tp = lax.axis_size("tp")
    core = lax.axis_index("core")
    tp_index = lax.axis_index("tp")
    width = model_width // (chips * cores * tp)
    plane = ("chip", "tp")
    swap = [(i, cores - 1 - i) for i in range(cores)]

    def both(weight):
        return [weight] + ([lax.ppermute(weight, "core", swap)] if cores == 2 else [])

    queries_w = both(w_query)
    keys_w = both(key_weight_matrix)
    values_w = both(value_weight_matrix)

    core_place = core.astype(jnp.int32).reshape(1)
    tp_place = tp_index.astype(jnp.int32).reshape(1)
    if width % 128 == 0:
        mine, scale = prepare(core_place, tp_place, hidden_in, norm_gain, chips, cores, tp)
    else:
        by_row = jnp.transpose(hidden_in, (1, 0, 2)).reshape(lines, model_width).astype(f32)
        blocked = (by_row * norm_gain.astype(f32)).astype(bf16)
        blocked = blocked.reshape(lines, chips, cores, tp, width)
        mine = lax.dynamic_index_in_dim(blocked, tp_index, 3, keepdims=False)
        if cores == 2:
            mine = jnp.where(core == 0, mine, mine[:, :, ::-1])
        mine = jnp.transpose(mine, (1, 2, 0, 3)).reshape(chips, cores * lines, width)
        scale = lax.rsqrt(jnp.mean(by_row * by_row, axis=-1, keepdims=True) + norm_eps)
        scale = jnp.broadcast_to(scale, (lines, 128))
    columns = lax.all_to_all(mine, "chip", split_axis=0, concat_axis=0, tiled=True)
    partials = qkv_partials(columns, list(zip(queries_w, keys_w, values_w)))
    late_out, partials = lax.optimization_barrier((w_out, partials))
    outs_w = both(late_out)
    parts = lax.all_to_all(partials, plane, split_axis=0, concat_axis=0, tiled=True)
    block = min(key_cache.shape[2], 4096)
    attended = attention(
        lengths,
        finished,
        parts,
        scale,
        (bias_query, key_bias_vector, value_bias_vector),
        key_cache,
        value_cache,
        chips * tp,
        block,
    )
    gathered = lax.all_to_all(attended, plane, split_axis=0, concat_axis=0, tiled=True)
    product = project(core_place, gathered, outs_w)
    arrived = lax.all_to_all(product, plane, split_axis=0, concat_axis=0, tiled=True)
    if width % 128 == 0:
        return finish(finished, arrived, hidden_in, cores)
    arrived = arrived.reshape(chips, tp, row_count, step_count, cores, width)
    projected = jnp.transpose(arrived, (3, 2, 0, 4, 1, 5)).reshape(
        step_count, row_count, model_width
    )
    hidden = hidden_in.astype(f32)
    layer_out = jnp.where(finished[None, :, None] != 0, hidden, hidden + projected.astype(f32))
    return layer_out.astype(bf16)


def solution(mesh):
    gen = mesh.shape["gen"]
    cores = 2 if gen % 2 == 0 else 1
    split = Mesh(
        mesh.devices.reshape(gen // cores, cores, mesh.shape["tp"]), ("chip", "core", "tp")
    )
    rows = ("chip", "core")
    every = ("chip", "core", "tp")
    placed = (
        P(None, rows, None),
        P(),
        P(every, None),
        P(every, None),
        P(every, None),
        P("tp"),
        P("tp"),
        P("tp"),
        P(None, every),
        P(rows, "tp", None, None),
        P(rows, "tp", None, None),
        P(rows),
        P(rows),
    )
    return jax.shard_map(
        shards, mesh=split, in_specs=placed, out_specs=P(None, rows, None), check_vma=False
    )
```

```python
import itertools
import math

import jax
import jax.numpy as jnp
from jax import lax
from jax.experimental import pallas as pl
from jax.experimental.pallas import tpu as pltpu
from jax.sharding import Mesh
from jax.sharding import PartitionSpec as P

norm_eps = 1e-06
rope_base = 1000000.0
masked_score = -1e30
bf16 = jnp.bfloat16
f32 = jnp.float32


whole = pl.BlockSpec(memory_space=pltpu.VMEM)
scalars = pl.BlockSpec(memory_space=pltpu.SMEM)
distant = pl.BlockSpec(memory_space=pltpu.HBM)


def far_away(array):
    return pltpu.with_memory_space_constraint(array, pltpu.HBM)


def params(mib):
    return pltpu.CompilerParams(vmem_limit_bytes=mib << 20)


def other_chip(chip, m, chips):
    if chips & (chips - 1) == 0:
        return chip ^ m
    return (m - chip) % chips


def slot_of(n, t, near, tp):
    return ((n // near) * tp + t) * near + n % near


def prepare(core, tp_index, chip, hidden_in, norm_gain, chips, cores, tp):
    step_count, row_count, model_width = hidden_in.shape
    lines = step_count * row_count
    width = model_width // (chips * cores * tp)

    def kernel(core_ref, tp_ref, chip_ref, h_hbm, g_hbm, *refs):
        mine_refs, scale_ref = refs[:chips], refs[chips]
        h_ref, g_ref, x_scr, g_scr, sems = refs[chips + 1 :]
        copies = [
            pltpu.make_async_copy(h_hbm, h_ref, sems.at[0]),
            pltpu.make_async_copy(g_hbm, g_ref, sems.at[1]),
        ]
        for copy in copies:
            copy.start()
        for copy in copies:
            copy.wait()
        for s in range(step_count):
            x = h_ref[s].astype(f32)
            for r in range(row_count):
                x_scr[r * step_count + s : r * step_count + s + 1, :] = x[r : r + 1]
        g_scr[...] = g_ref[...].astype(f32)
        own = core_ref[0]
        for m in range(chips):
            n = other_chip(chip_ref[0], m, chips)
            for c in range(cores):
                at = own if c == 0 else 1 - own
                block = ((n * cores + at) * tp + tp_ref[0]) * (width // 128)
                for b in range(width // 128):
                    start = pl.multiple_of((block + b) * 128, 128)
                    x = x_scr[:, pl.ds(start, 128)] * g_scr[pl.ds(block + b, 1), :]
                    mine_refs[m][c * lines : (c + 1) * lines, b * 128 : (b + 1) * 128] = x.astype(
                        bf16
                    )
        square = jnp.zeros((lines, 128), f32)
        for b in range(model_width // 128):
            x = x_scr[:, b * 128 : (b + 1) * 128]
            square = square + x * x
        mean = jnp.sum(square, axis=1, keepdims=True) * (1.0 / model_width)
        scale_ref[...] = jnp.broadcast_to(lax.rsqrt(mean + norm_eps), (lines, 128))

    return pl.pallas_call(
        kernel,
        out_shape=(jax.ShapeDtypeStruct((cores * lines, width), bf16),) * chips
        + (jax.ShapeDtypeStruct((lines, 128), f32),),
        in_specs=[scalars, scalars, scalars, distant, distant],
        out_specs=(whole,) * (chips + 1),
        scratch_shapes=[
            pltpu.VMEM(hidden_in.shape, bf16),
            pltpu.VMEM((model_width // 128, 128), bf16),
            pltpu.VMEM((lines, model_width), f32),
            pltpu.VMEM((model_width // 128, 128), f32),
            pltpu.SemaphoreType.DMA((2,)),
        ],
        compiler_params=params(4),
        name="prepare",
    )(
        core,
        tp_index,
        chip,
        far_away(hidden_in),
        far_away(norm_gain.reshape(model_width // 128, 128)),
    )


def staged(arrays, after):
    count = len(arrays)

    def kernel(*refs):
        sources, outs, sems = refs[:count], refs[count + 1 : 2 * count + 1], refs[-1]
        copies = [pltpu.make_async_copy(sources[i], outs[i], sems.at[i]) for i in range(count)]
        for copy in copies:
            copy.start()
        for copy in copies:
            copy.wait()

    return pl.pallas_call(
        kernel,
        out_shape=tuple(pltpu.VMEM(a.shape, a.dtype) for a in arrays),
        in_specs=[distant] * count + [pl.BlockSpec(memory_space=pl.ANY)],
        out_specs=(whole,) * count,
        scratch_shapes=[pltpu.SemaphoreType.DMA((count,))],
        compiler_params=params(1),
        cost_estimate=pl.CostEstimate(
            flops=0, bytes_accessed=sum(math.prod(a.shape) * 2 for a in arrays), transcendentals=0
        ),
        name="stage_weights",
    )(*[far_away(a) for a in arrays], after)


def qkv_partials(chip, columns, weights, near, tp):
    chips = len(columns)
    depth, width = columns[0].shape
    cores = len(weights)
    per = depth // cores
    rows = chips * per
    sizes = [w.shape[1] // tp for w in weights[0]]
    total = sum(sizes)
    flat = [w for group in weights for w in group]

    def kernel(chip_ref, *refs):
        x_refs, w_refs, out_ref = refs[:chips], refs[chips:-1], refs[-1]
        lhs = [
            jnp.concatenate([x[c * per : (c + 1) * per] for x in x_refs], axis=0)
            for c in range(cores)
        ]
        places = [other_chip(chip_ref[0], m, chips) for m in range(chips)]
        for t in range(tp):
            slots = [slot_of(n, t, near, tp) for n in places]
            start = 0
            for kind, size in enumerate(sizes):
                acc = None
                for c in range(cores):
                    w = w_refs[c * 3 + kind][:, t * size : (t + 1) * size]
                    part = jnp.dot(lhs[c], w, preferred_element_type=f32)
                    acc = part if acc is None else acc + part
                acc = acc.astype(bf16)
                for m in range(chips):
                    out_ref[slots[m], :, start : start + size] = acc[m * per : (m + 1) * per]
                start += size

    return pl.pallas_call(
        kernel,
        out_shape=pltpu.VMEM((chips * tp, per, total), bf16),
        in_specs=[scalars] + [whole] * (chips + len(flat)),
        out_specs=whole,
        compiler_params=params(6),
        cost_estimate=pl.CostEstimate(
            flops=2 * cores * rows * width * total * tp,
            bytes_accessed=2 * cores * width * total * tp,
            transcendentals=0,
        ),
        name="qkv_partials",
    )(chip, *columns, *flat)


def attention(lengths, finished, parts, scale, biases, key_cache, value_cache, copies, block):
    sources, lines, total = parts.shape
    row_count, kv_heads, cache_len, head_dim = key_cache.shape
    steps = lines // row_count
    kv_width = kv_heads * head_dim
    q_width = total - 2 * kv_width
    heads = q_width // head_dim
    group = heads // kv_heads
    queries = group * steps
    fresh = 8
    small = min(block, 1024)
    factor = math.log2(math.e) / math.sqrt(head_dim)
    pairs = [(r, j) for r in range(row_count) for j in range(kv_heads)]

    def kernel(length_ref, finished_ref, p_ref, scale_ref, bq_ref, bk_ref, bv_ref, k_ref, v_ref,
               out_ref, k_scr, v_scr, q_scr, kn_scr, vn_scr, s_scr, o_scr, sems):
        lives = [
            jnp.where(finished_ref[r] != 0, 0, length_ref[r]) for r in range(row_count)
        ]
        larges = [length // block for length in lives]
        smalls = [
            (length - large * block + small - 1) // small for length, large in zip(lives, larges)
        ]
        tails = [large * block for large in larges]

        def fetch(r, kind, sem, start, size):
            source, target = ((k_ref, k_scr), (v_ref, v_scr))[kind]
            part = pl.ds(start, size)
            return pltpu.make_async_copy(
                source.at[r, :, part, :], target.at[r, :, part, :], sems.at[r, kind, sem]
            )

        def large_at(r, i):
            return pl.multiple_of(i * block, block)

        def small_at(r, i):
            return pl.multiple_of(tails[r] + i * small, small)

        most_large = cache_len // block

        for r in range(row_count):
            for kind in range(2):
                def start_large(i, carry):
                    fetch(r, kind, i, large_at(r, i), block).start()
                    return carry

                def start_small(i, carry):
                    fetch(r, kind, most_large + i, small_at(r, i), small).start()
                    return carry

                lax.fori_loop(0, larges[r], start_large, 0)
                lax.fori_loop(0, smalls[r], start_small, 0)
        scale = scale_ref[...]
        line = lax.broadcasted_iota(jnp.int32, (lines, head_dim), 0)
        lane = lax.broadcasted_iota(jnp.int32, (lines, head_dim), 1)
        position = line % steps
        for r in range(row_count):
            position = position + jnp.where(line // steps == r, length_ref[r], 0)
        half = head_dim // 2
        pair = (lane % half).astype(f32)
        frequency = jnp.exp(pair * (-2.0 * math.log(rope_base) / head_dim))
        angles = position.astype(f32) * frequency
        cos = jnp.cos(angles)
        sin = jnp.where(lane < half, -1.0, 1.0) * jnp.sin(angles)

        def summed(start, bias_row):
            terms = [p_ref[i, :, start : start + head_dim].astype(f32) for i in range(sources)]
            while len(terms) > 1:
                terms = [sum(terms[i : i + 2]) for i in range(0, len(terms), 2)]
            return terms[0] * scale + bias_row.astype(f32)

        def rotated(start, bias_row):
            head = summed(start, bias_row)
            return head * cos + pltpu.roll(head, half, 1) * sin

        kn_scr[...] = jnp.zeros_like(kn_scr)
        vn_scr[...] = jnp.zeros_like(vn_scr)
        for h in range(heads):
            q = rotated(h * head_dim, bq_ref[h : h + 1, :])
            for r in range(row_count):
                g = h % group
                q_scr[r, h // group, g * steps : (g + 1) * steps, :] = q[r * steps : (r + 1) * steps]
        for j in range(kv_heads):
            k = rotated(q_width + j * head_dim, bk_ref[j : j + 1, :])
            v = summed(q_width + kv_width + j * head_dim, bv_ref[j : j + 1, :])
            for r in range(row_count):
                kn_scr[r, j, 0:steps, :] = k[r * steps : (r + 1) * steps]
                vn_scr[r, j, 0:steps, :] = v[r * steps : (r + 1) * steps]
        step_of = lax.broadcasted_iota(jnp.int32, (queries, fresh), 0) % steps
        allowed = lax.broadcasted_iota(jnp.int32, (queries, fresh), 1) <= step_of
        nt = (((1,), (1,)), ((), ()))
        qs = {}
        new_scores = {}
        new_tops = {}
        for r, j in pairs:
            qs[r, j] = q_scr[r, j].astype(bf16)
            s = lax.dot_general(
                qs[r, j], kn_scr[r, j].astype(bf16), nt, preferred_element_type=f32
            )
            new_scores[r, j] = jnp.where(allowed, s, masked_score)
            new_tops[r, j] = jnp.max(new_scores[r, j], axis=1, keepdims=True)
        tops = {}
        lane_sums = {}
        totals = {}
        for r in range(row_count):

            def scores(start, size, masked, most):
                out = []
                for j in range(kv_heads):
                    s = lax.dot_general(
                        qs[r, j], k_scr[r, j, pl.ds(start, size), :], nt, preferred_element_type=f32
                    )
                    if masked:
                        place = start + lax.broadcasted_iota(jnp.int32, (queries, size), 1)
                        s = jnp.where(place < lives[r], s, masked_score)
                    s_scr[j, :, pl.ds(start, size)] = s
                    top = most[j]
                    for b in range(size // 128):
                        top = jnp.maximum(top, s[:, b * 128 : (b + 1) * 128])
                    out.append(top)
                return tuple(out)

            def score_large(i, most):
                start = large_at(r, i)
                fetch(r, 0, i, start, block).wait()
                return scores(start, block, False, most)

            def score_small(i, most):
                start = small_at(r, i)
                fetch(r, 0, most_large + i, start, small).wait()
                return scores(start, small, True, most)

            most = tuple(jnp.full((queries, 128), masked_score, f32) for _ in range(kv_heads))
            most = lax.fori_loop(0, larges[r], score_large, most)
            most = lax.fori_loop(0, smalls[r], score_small, most)
            for j in range(kv_heads):
                tops[r, j] = jnp.maximum(
                    jnp.max(most[j], axis=1, keepdims=True), new_tops[r, j]
                )

            def gather(start, size, carry):
                lanes, accs = carry
                new_lanes = []
                new_accs = []
                for j in range(kv_heads):
                    p = jnp.exp2((s_scr[j, :, pl.ds(start, size)] - tops[r, j]) * factor)
                    lane_sum = lanes[j]
                    for b in range(size // 128):
                        lane_sum = lane_sum + p[:, b * 128 : (b + 1) * 128]
                    new_lanes.append(lane_sum)
                    new_accs.append(
                        accs[j]
                        + jnp.dot(
                            p.astype(bf16),
                            v_scr[r, j, pl.ds(start, size), :],
                            preferred_element_type=f32,
                        )
                    )
                return tuple(new_lanes), tuple(new_accs)

            def gather_large(i, carry):
                start = large_at(r, i)
                fetch(r, 1, i, start, block).wait()
                return gather(start, block, carry)

            def gather_small(i, carry):
                start = small_at(r, i)
                fetch(r, 1, most_large + i, start, small).wait()
                return gather(start, small, carry)

            carry = (
                tuple(jnp.zeros((queries, 128), f32) for _ in range(kv_heads)),
                tuple(jnp.zeros((queries, head_dim), f32) for _ in range(kv_heads)),
            )
            carry = lax.fori_loop(0, larges[r], gather_large, carry)
            carry = lax.fori_loop(0, smalls[r], gather_small, carry)
            for j in range(kv_heads):
                lane_sums[r, j] = carry[0][j]
                totals[r, j] = carry[1][j]
        for r, j in pairs:
            p = jnp.exp2((new_scores[r, j] - tops[r, j]) * factor)
            total_sum = jnp.sum(lane_sums[r, j], axis=1, keepdims=True) + jnp.sum(
                p, axis=1, keepdims=True
            )
            o = totals[r, j] + jnp.dot(
                p.astype(bf16), vn_scr[r, j].astype(bf16), preferred_element_type=f32
            )
            o = o / total_sum
            for g in range(group):
                col = (j * group + g) * head_dim
                o_scr[r * steps : (r + 1) * steps, col : col + head_dim] = o[
                    g * steps : (g + 1) * steps
                ]
        result = o_scr[...].astype(bf16)
        for n in range(copies):
            out_ref[n] = result

    flops = 4 * row_count * kv_heads * queries * cache_len * head_dim
    return pl.pallas_call(
        kernel,
        out_shape=pltpu.VMEM((copies, lines, q_width), bf16),
        in_specs=[scalars, scalars] + [whole] * 5 + [distant] * 2,
        out_specs=whole,
        scratch_shapes=[
            pltpu.VMEM(key_cache.shape, bf16),
            pltpu.VMEM(value_cache.shape, bf16),
            pltpu.VMEM((row_count, kv_heads, queries, head_dim), f32),
            pltpu.VMEM((row_count, kv_heads, fresh, head_dim), f32),
            pltpu.VMEM((row_count, kv_heads, fresh, head_dim), f32),
            pltpu.VMEM((kv_heads, queries, cache_len), f32),
            pltpu.VMEM((lines, q_width), f32),
            pltpu.SemaphoreType.DMA((row_count, 2, cache_len // block + block // small)),
        ],
        compiler_params=params(48),
        cost_estimate=pl.CostEstimate(
            flops=flops,
            bytes_accessed=4 * row_count * kv_heads * cache_len * head_dim,
            transcendentals=0,
        ),
        name="attention",
    )(
        lengths,
        finished,
        parts,
        scale,
        *[b.reshape(-1, head_dim) for b in biases],
        far_away(key_cache),
        far_away(value_cache),
    )


def project(core, gathered, weights, near, tp):
    sources, per, width = gathered.shape
    chips = sources // tp
    cores = len(weights)
    columns = weights[0].shape[1]

    def kernel(core_ref, a_ref, near_ref, *refs):
        far = refs[: cores - 1]
        out_ref, held, sems = refs[cores - 1], refs[cores : 2 * cores - 1], refs[-1]
        first = core_ref[0] == 0
        copies = []
        for t in range(tp):
            part = pl.ds(t * width, width)
            for c in range(cores - 1):
                copies.append(
                    pltpu.make_async_copy(far[c].at[part, :], held[c].at[part, :], sems.at[t])
                )
                copies[-1].start()
        lhs = [
            jnp.concatenate([a_ref[slot_of(n, t, near, tp)] for n in range(chips)], axis=0)
            for t in range(tp)
        ]
        accs = []
        for c in range(cores):
            acc = None
            for t in range(tp):
                source = near_ref
                if c:
                    copies[t].wait()
                    source = held[c - 1]
                part = jnp.dot(
                    lhs[t], source[t * width : (t + 1) * width, :], preferred_element_type=f32
                )
                acc = part if acc is None else acc + part
            accs.append(acc)
        if cores == 2:
            accs = [jnp.where(first, accs[0], accs[1]), jnp.where(first, accs[1], accs[0])]
        acc = jnp.concatenate(accs, axis=1).astype(bf16)
        for n in range(chips):
            for t in range(tp):
                out_ref[slot_of(n, t, near, tp)] = acc[n * per : (n + 1) * per]

    return pl.pallas_call(
        kernel,
        out_shape=pltpu.VMEM((sources, per, cores * columns), bf16),
        in_specs=[scalars, whole, whole] + [distant] * (cores - 1),
        out_specs=whole,
        scratch_shapes=[pltpu.VMEM(w.shape, w.dtype) for w in weights[1:]]
        + [pltpu.SemaphoreType.DMA((tp,))],
        compiler_params=params(8),
        cost_estimate=pl.CostEstimate(
            flops=2 * chips * per * tp * width * cores * columns,
            bytes_accessed=2 * tp * width * cores * columns,
            transcendentals=0,
        ),
        name="project",
    )(core, gathered, *weights)


def finish(finished, arrived, hidden_in, cores, near, tp):
    sources, lines, wide = arrived.shape
    step_count, row_count, model_width = hidden_in.shape
    chips = sources // tp
    width = wide // cores

    def kernel(finished_ref, a_ref, h_ref, out_ref, y_scr):
        for n, t, c in itertools.product(range(chips), range(tp), range(cores)):
            start = ((n * cores + c) * tp + t) * width
            part = a_ref[slot_of(n, t, near, tp), :, c * width : (c + 1) * width]
            y_scr[:, start : start + width] = part.astype(f32)
        row = lax.broadcasted_iota(jnp.int32, (row_count, 1), 0)
        done = jnp.zeros((row_count, 1), jnp.int32)
        for r in range(row_count):
            done = jnp.where(row == r, finished_ref[r], done)
        for s in range(step_count):
            hidden = h_ref[s].astype(f32)
            lines_of = [r * step_count + s for r in range(row_count)]
            moved = hidden + jnp.concatenate([y_scr[i : i + 1, :] for i in lines_of], axis=0)
            out_ref[s] = jnp.where(done != 0, hidden, moved).astype(bf16)

    return pl.pallas_call(
        kernel,
        out_shape=jax.ShapeDtypeStruct(hidden_in.shape, bf16),
        in_specs=[scalars, whole, whole],
        out_specs=whole,
        scratch_shapes=[pltpu.VMEM((lines, model_width), f32)],
        compiler_params=params(4),
        name="finish",
    )(finished, arrived, hidden_in)


def shards(
    hidden_in,
    norm_gain,
    w_query,
    key_weight_matrix,
    value_weight_matrix,
    bias_query,
    key_bias_vector,
    value_bias_vector,
    w_out,
    key_cache,
    value_cache,
    lengths,
    finished,
):
    step_count, row_count, model_width = hidden_in.shape
    lines = step_count * row_count
    head_dim = key_cache.shape[3]
    near = lax.axis_size("near")
    chips = lax.axis_size("far") * near
    chip_axes = ("far", "near")
    chip = lax.axis_index(chip_axes)
    cores = lax.axis_size("core")
    tp = lax.axis_size("tp")
    core = lax.axis_index("core")
    tp_index = lax.axis_index("tp")
    width = model_width // (chips * cores * tp)
    plane = ("far", "tp", "near")
    swap = [(i, cores - 1 - i) for i in range(cores)]

    def both(weight):
        return [weight] + ([lax.ppermute(weight, "core", swap)] if cores == 2 else [])

    queries_w = both(w_query)
    keys_w = both(key_weight_matrix)
    values_w = both(value_weight_matrix)

    core_place = core.astype(jnp.int32).reshape(1)
    tp_place = tp_index.astype(jnp.int32).reshape(1)
    chip_place = chip.astype(jnp.int32).reshape(1)
    if width % 128 == 0:
        *mine, scale = prepare(
            core_place, tp_place, chip_place, hidden_in, norm_gain, chips, cores, tp
        )
    else:
        by_row = jnp.transpose(hidden_in, (1, 0, 2)).reshape(lines, model_width).astype(f32)
        blocked = (by_row * norm_gain.astype(f32)).astype(bf16)
        blocked = blocked.reshape(lines, chips, cores, tp, width)
        mine = lax.dynamic_index_in_dim(blocked, tp_index, 3, keepdims=False)
        if cores == 2:
            mine = jnp.where(core == 0, mine, mine[:, :, ::-1])
        mine = jnp.transpose(mine, (1, 2, 0, 3)).reshape(chips, cores * lines, width)
        mine = [
            lax.dynamic_index_in_dim(mine, other_chip(chip, m, chips), 0, keepdims=False)
            for m in range(chips)
        ]
        scale = lax.rsqrt(jnp.mean(by_row * by_row, axis=-1, keepdims=True) + norm_eps)
        scale = jnp.broadcast_to(scale, (lines, 128))
    columns = []
    for m in range(chips):
        pairs = [(i, other_chip(i, m, chips)) for i in range(chips)]
        still = all(i == j for i, j in pairs)
        columns.append(mine[m] if still else lax.ppermute(mine[m], chip_axes, pairs))
    held = staged((w_query, key_weight_matrix, value_weight_matrix), mine[0])
    weights = [held] + list(zip(queries_w, keys_w, values_w))[1:]
    partials = qkv_partials(chip_place, columns, weights, near, tp)
    late_out, partials = lax.optimization_barrier((w_out, partials))
    outs_w = both(late_out)
    parts = lax.all_to_all(partials, plane, split_axis=0, concat_axis=0, tiled=True)
    block = min(key_cache.shape[2], 4096)
    attended = attention(
        lengths,
        finished,
        parts,
        scale,
        (bias_query, key_bias_vector, value_bias_vector),
        key_cache,
        value_cache,
        chips * tp,
        block,
    )
    gathered = lax.all_to_all(attended, plane, split_axis=0, concat_axis=0, tiled=True)
    product = project(core_place, gathered, outs_w, near, tp)
    arrived = lax.all_to_all(product, plane, split_axis=0, concat_axis=0, tiled=True)
    if width % 128 == 0:
        return finish(finished, arrived, hidden_in, cores, near, tp)
    arrived = arrived.reshape(chips // near, tp, near, row_count, step_count, cores, width)
    projected = jnp.transpose(arrived, (4, 3, 0, 2, 5, 1, 6)).reshape(
        step_count, row_count, model_width
    )
    hidden = hidden_in.astype(f32)
    layer_out = jnp.where(finished[None, :, None] != 0, hidden, hidden + projected.astype(f32))
    return layer_out.astype(bf16)


def solution(mesh):
    gen = mesh.shape["gen"]
    cores = 2 if gen % 2 == 0 else 1
    chips = gen // cores
    near = 2 if chips % 2 == 0 else 1
    split = Mesh(
        mesh.devices.reshape(chips // near, near, cores, mesh.shape["tp"]),
        ("far", "near", "core", "tp"),
    )
    rows = ("far", "near", "core")
    every = rows + ("tp",)
    placed = (
        P(None, rows, None),
        P(),
        P(every, None),
        P(every, None),
        P(every, None),
        P("tp"),
        P("tp"),
        P("tp"),
        P(None, every),
        P(rows, "tp", None, None),
        P(rows, "tp", None, None),
        P(rows),
        P(rows),
    )
    return jax.shard_map(
        shards, mesh=split, in_specs=placed, out_specs=P(None, rows, None), check_vma=False
    )
```

```python
import itertools
import math

import jax
import jax.numpy as jnp
from jax import lax
from jax.experimental import pallas as pl
from jax.experimental.pallas import tpu as pltpu
from jax.sharding import Mesh
from jax.sharding import PartitionSpec as P

norm_eps = 1e-06
rope_base = 1000000.0
masked_score = -1e30
bf16 = jnp.bfloat16
f32 = jnp.float32


whole = pl.BlockSpec(memory_space=pltpu.VMEM)
scalars = pl.BlockSpec(memory_space=pltpu.SMEM)
distant = pl.BlockSpec(memory_space=pltpu.HBM)


def far_away(array):
    return pltpu.with_memory_space_constraint(array, pltpu.HBM)


def params(mib):
    return pltpu.CompilerParams(vmem_limit_bytes=mib << 20)


def other_chip(chip, m, chips):
    if chips & (chips - 1) == 0:
        return chip ^ m
    return (m - chip) % chips


def slot_of(n, t, near, tp):
    return ((n // near) * tp + t) * near + n % near


def prepare(core, tp_index, chip, hidden_in, norm_gain, chips, cores, tp):
    step_count, row_count, model_width = hidden_in.shape
    lines = step_count * row_count
    width = model_width // (chips * cores * tp)

    def kernel(core_ref, tp_ref, chip_ref, h_hbm, g_hbm, *refs):
        mine_refs, scale_ref, x_ref = refs[:chips], refs[chips], refs[chips + 1]
        h_ref, g_ref, g_scr, sems = refs[chips + 2 :]
        copies = [
            pltpu.make_async_copy(h_hbm, h_ref, sems.at[0]),
            pltpu.make_async_copy(g_hbm, g_ref, sems.at[1]),
        ]
        for copy in copies:
            copy.start()
        for copy in copies:
            copy.wait()
        for s in range(step_count):
            for b in range(model_width // 128):
                x_ref[b, pl.ds(s, row_count, stride=step_count), :] = h_ref[
                    s, :, b * 128 : (b + 1) * 128
                ].astype(f32)
        g_scr[...] = g_ref[...].astype(f32)
        own = core_ref[0]
        for m in range(chips):
            n = other_chip(chip_ref[0], m, chips)
            for c in range(cores):
                at = own if c == 0 else 1 - own
                block = ((n * cores + at) * tp + tp_ref[0]) * (width // 128)
                for b in range(width // 128):
                    x = x_ref[block + b] * g_scr[pl.ds(block + b, 1), :]
                    mine_refs[m][c * lines : (c + 1) * lines, b * 128 : (b + 1) * 128] = x.astype(
                        bf16
                    )
        square = jnp.zeros((lines, 128), f32)
        for b in range(model_width // 128):
            square = square + x_ref[b] * x_ref[b]
        mean = jnp.sum(square, axis=1, keepdims=True) * (1.0 / model_width)
        scale_ref[...] = jnp.broadcast_to(lax.rsqrt(mean + norm_eps), (lines, 128))

    return pl.pallas_call(
        kernel,
        out_shape=(jax.ShapeDtypeStruct((cores * lines, width), bf16),) * chips
        + (
            jax.ShapeDtypeStruct((lines, 128), f32),
            pltpu.VMEM((model_width // 128, lines, 128), f32),
        ),
        in_specs=[scalars, scalars, scalars, distant, distant],
        out_specs=(whole,) * (chips + 2),
        scratch_shapes=[
            pltpu.VMEM(hidden_in.shape, bf16),
            pltpu.VMEM((model_width // 128, 128), bf16),
            pltpu.VMEM((model_width // 128, 128), f32),
            pltpu.SemaphoreType.DMA((2,)),
        ],
        compiler_params=params(4),
        name="prepare",
    )(
        core,
        tp_index,
        chip,
        far_away(hidden_in),
        far_away(norm_gain.reshape(model_width // 128, 128)),
    )


def staged(arrays, after):
    count = len(arrays)

    def kernel(*refs):
        sources, outs, sems = refs[:count], refs[count + 1 : 2 * count + 1], refs[-1]
        copies = [pltpu.make_async_copy(sources[i], outs[i], sems.at[i]) for i in range(count)]
        for copy in copies:
            copy.start()
        for copy in copies:
            copy.wait()

    return pl.pallas_call(
        kernel,
        out_shape=tuple(pltpu.VMEM(a.shape, a.dtype) for a in arrays),
        in_specs=[distant] * count + [pl.BlockSpec(memory_space=pl.ANY)],
        out_specs=(whole,) * count,
        scratch_shapes=[pltpu.SemaphoreType.DMA((count,))],
        compiler_params=params(1),
        cost_estimate=pl.CostEstimate(
            flops=0, bytes_accessed=sum(math.prod(a.shape) * 2 for a in arrays), transcendentals=0
        ),
        name="stage_weights",
    )(*[far_away(a) for a in arrays], after)


def qkv_partials(chip, columns, weights, near, tp):
    chips = len(columns)
    depth, width = columns[0].shape
    cores = len(weights)
    per = depth // cores
    rows = chips * per
    sizes = [w.shape[1] // tp for w in weights[0]]
    total = sum(sizes)
    flat = [w for group in weights for w in group]

    def kernel(chip_ref, *refs):
        x_refs, w_refs, out_ref = refs[:chips], refs[chips:-1], refs[-1]
        lhs = [
            jnp.concatenate([x[c * per : (c + 1) * per] for x in x_refs], axis=0)
            for c in range(cores)
        ]
        places = [other_chip(chip_ref[0], m, chips) for m in range(chips)]
        for t in range(tp):
            slots = [slot_of(n, t, near, tp) for n in places]
            start = 0
            for kind, size in enumerate(sizes):
                acc = None
                for c in range(cores):
                    w = w_refs[c * 3 + kind][:, t * size : (t + 1) * size]
                    part = jnp.dot(lhs[c], w, preferred_element_type=f32)
                    acc = part if acc is None else acc + part
                acc = acc.astype(bf16)
                for m in range(chips):
                    out_ref[slots[m], :, start : start + size] = acc[m * per : (m + 1) * per]
                start += size

    return pl.pallas_call(
        kernel,
        out_shape=pltpu.VMEM((chips * tp, per, total), bf16),
        in_specs=[scalars] + [whole] * (chips + len(flat)),
        out_specs=whole,
        compiler_params=params(6),
        cost_estimate=pl.CostEstimate(
            flops=2 * cores * rows * width * total * tp,
            bytes_accessed=2 * cores * width * total * tp,
            transcendentals=0,
        ),
        name="qkv_partials",
    )(chip, *columns, *flat)


def attention(lengths, finished, parts, scale, biases, key_cache, value_cache, copies, block):
    sources, lines, total = parts.shape
    row_count, kv_heads, cache_len, head_dim = key_cache.shape
    steps = lines // row_count
    kv_width = kv_heads * head_dim
    q_width = total - 2 * kv_width
    heads = q_width // head_dim
    group = heads // kv_heads
    queries = group * steps
    fresh = 8
    small = min(block, 1024)
    factor = math.log2(math.e) / math.sqrt(head_dim)
    pairs = [(r, j) for r in range(row_count) for j in range(kv_heads)]

    def kernel(length_ref, finished_ref, p_ref, scale_ref, bq_ref, bk_ref, bv_ref, k_ref, v_ref,
               out_ref, k_scr, v_scr, q_scr, kn_scr, vn_scr, s_scr, o_scr, sems):
        lives = [
            jnp.where(finished_ref[r] != 0, 0, length_ref[r]) for r in range(row_count)
        ]
        larges = [length // block for length in lives]
        smalls = [
            (length - large * block + small - 1) // small for length, large in zip(lives, larges)
        ]
        tails = [large * block for large in larges]

        def fetch(r, kind, sem, start, size):
            source, target = ((k_ref, k_scr), (v_ref, v_scr))[kind]
            part = pl.ds(start, size)
            return pltpu.make_async_copy(
                source.at[r, :, part, :], target.at[r, :, part, :], sems.at[r, kind, sem]
            )

        def large_at(r, i):
            return pl.multiple_of(i * block, block)

        def small_at(r, i):
            return pl.multiple_of(tails[r] + i * small, small)

        most_large = cache_len // block

        for r in range(row_count):
            for kind in range(2):
                def start_large(i, carry):
                    fetch(r, kind, i, large_at(r, i), block).start()
                    return carry

                def start_small(i, carry):
                    fetch(r, kind, most_large + i, small_at(r, i), small).start()
                    return carry

                lax.fori_loop(0, larges[r], start_large, 0)
                lax.fori_loop(0, smalls[r], start_small, 0)
        scale = scale_ref[...]
        line = lax.broadcasted_iota(jnp.int32, (lines, head_dim), 0)
        lane = lax.broadcasted_iota(jnp.int32, (lines, head_dim), 1)
        position = line % steps
        for r in range(row_count):
            position = position + jnp.where(line // steps == r, length_ref[r], 0)
        half = head_dim // 2
        pair = (lane % half).astype(f32)
        frequency = jnp.exp(pair * (-2.0 * math.log(rope_base) / head_dim))
        angles = position.astype(f32) * frequency
        cos = jnp.cos(angles)
        sin = jnp.where(lane < half, -1.0, 1.0) * jnp.sin(angles)

        def summed(start, bias_row):
            terms = [p_ref[i, :, start : start + head_dim].astype(f32) for i in range(sources)]
            while len(terms) > 1:
                terms = [sum(terms[i : i + 2]) for i in range(0, len(terms), 2)]
            return terms[0] * scale + bias_row.astype(f32)

        def rotated(start, bias_row):
            head = summed(start, bias_row)
            return head * cos + pltpu.roll(head, half, 1) * sin

        kn_scr[...] = jnp.zeros_like(kn_scr)
        vn_scr[...] = jnp.zeros_like(vn_scr)
        for h in range(heads):
            q = rotated(h * head_dim, bq_ref[h : h + 1, :])
            for r in range(row_count):
                g = h % group
                q_scr[r, h // group, g * steps : (g + 1) * steps, :] = q[r * steps : (r + 1) * steps]
        for j in range(kv_heads):
            k = rotated(q_width + j * head_dim, bk_ref[j : j + 1, :])
            v = summed(q_width + kv_width + j * head_dim, bv_ref[j : j + 1, :])
            for r in range(row_count):
                kn_scr[r, j, 0:steps, :] = k[r * steps : (r + 1) * steps]
                vn_scr[r, j, 0:steps, :] = v[r * steps : (r + 1) * steps]
        step_of = lax.broadcasted_iota(jnp.int32, (queries, fresh), 0) % steps
        allowed = lax.broadcasted_iota(jnp.int32, (queries, fresh), 1) <= step_of
        nt = (((1,), (1,)), ((), ()))
        qs = {}
        new_scores = {}
        new_tops = {}
        for r, j in pairs:
            qs[r, j] = q_scr[r, j].astype(bf16)
            s = lax.dot_general(
                qs[r, j], kn_scr[r, j].astype(bf16), nt, preferred_element_type=f32
            )
            new_scores[r, j] = jnp.where(allowed, s, masked_score)
            new_tops[r, j] = jnp.max(new_scores[r, j], axis=1, keepdims=True)
        tops = {}
        lane_sums = {}
        totals = {}
        for r in range(row_count):

            def scores(start, size, masked, most):
                out = []
                for j in range(kv_heads):
                    s = lax.dot_general(
                        qs[r, j], k_scr[r, j, pl.ds(start, size), :], nt, preferred_element_type=f32
                    )
                    if masked:
                        place = start + lax.broadcasted_iota(jnp.int32, (queries, size), 1)
                        s = jnp.where(place < lives[r], s, masked_score)
                    s_scr[j, :, pl.ds(start, size)] = s
                    top = most[j]
                    for b in range(size // 128):
                        top = jnp.maximum(top, s[:, b * 128 : (b + 1) * 128])
                    out.append(top)
                return tuple(out)

            def score_large(i, most):
                start = large_at(r, i)
                fetch(r, 0, i, start, block).wait()
                return scores(start, block, False, most)

            def score_small(i, most):
                start = small_at(r, i)
                fetch(r, 0, most_large + i, start, small).wait()
                return scores(start, small, True, most)

            most = tuple(jnp.full((queries, 128), masked_score, f32) for _ in range(kv_heads))
            most = lax.fori_loop(0, larges[r], score_large, most)
            most = lax.fori_loop(0, smalls[r], score_small, most)
            for j in range(kv_heads):
                tops[r, j] = jnp.maximum(
                    jnp.max(most[j], axis=1, keepdims=True), new_tops[r, j]
                )

            def gather(start, size, carry):
                lanes, accs = carry
                new_lanes = []
                new_accs = []
                for j in range(kv_heads):
                    p = jnp.exp2((s_scr[j, :, pl.ds(start, size)] - tops[r, j]) * factor)
                    lane_sum = lanes[j]
                    for b in range(size // 128):
                        lane_sum = lane_sum + p[:, b * 128 : (b + 1) * 128]
                    new_lanes.append(lane_sum)
                    new_accs.append(
                        accs[j]
                        + jnp.dot(
                            p.astype(bf16),
                            v_scr[r, j, pl.ds(start, size), :],
                            preferred_element_type=f32,
                        )
                    )
                return tuple(new_lanes), tuple(new_accs)

            def gather_large(i, carry):
                start = large_at(r, i)
                fetch(r, 1, i, start, block).wait()
                return gather(start, block, carry)

            def gather_small(i, carry):
                start = small_at(r, i)
                fetch(r, 1, most_large + i, start, small).wait()
                return gather(start, small, carry)

            carry = (
                tuple(jnp.zeros((queries, 128), f32) for _ in range(kv_heads)),
                tuple(jnp.zeros((queries, head_dim), f32) for _ in range(kv_heads)),
            )
            carry = lax.fori_loop(0, larges[r], gather_large, carry)
            carry = lax.fori_loop(0, smalls[r], gather_small, carry)
            for j in range(kv_heads):
                lane_sums[r, j] = carry[0][j]
                totals[r, j] = carry[1][j]
        for r, j in pairs:
            p = jnp.exp2((new_scores[r, j] - tops[r, j]) * factor)
            total_sum = jnp.sum(lane_sums[r, j], axis=1, keepdims=True) + jnp.sum(
                p, axis=1, keepdims=True
            )
            o = totals[r, j] + jnp.dot(
                p.astype(bf16), vn_scr[r, j].astype(bf16), preferred_element_type=f32
            )
            o = o / total_sum
            for g in range(group):
                col = (j * group + g) * head_dim
                o_scr[r * steps : (r + 1) * steps, col : col + head_dim] = o[
                    g * steps : (g + 1) * steps
                ]
        result = o_scr[...].astype(bf16)
        for n in range(copies):
            out_ref[n] = result

    flops = 4 * row_count * kv_heads * queries * cache_len * head_dim
    return pl.pallas_call(
        kernel,
        out_shape=pltpu.VMEM((copies, lines, q_width), bf16),
        in_specs=[scalars, scalars] + [whole] * 5 + [distant] * 2,
        out_specs=whole,
        scratch_shapes=[
            pltpu.VMEM(key_cache.shape, bf16),
            pltpu.VMEM(value_cache.shape, bf16),
            pltpu.VMEM((row_count, kv_heads, queries, head_dim), f32),
            pltpu.VMEM((row_count, kv_heads, fresh, head_dim), f32),
            pltpu.VMEM((row_count, kv_heads, fresh, head_dim), f32),
            pltpu.VMEM((kv_heads, queries, cache_len), f32),
            pltpu.VMEM((lines, q_width), f32),
            pltpu.SemaphoreType.DMA((row_count, 2, cache_len // block + block // small)),
        ],
        compiler_params=params(48),
        cost_estimate=pl.CostEstimate(
            flops=flops,
            bytes_accessed=4 * row_count * kv_heads * cache_len * head_dim,
            transcendentals=0,
        ),
        name="attention",
    )(
        lengths,
        finished,
        parts,
        scale,
        *[b.reshape(-1, head_dim) for b in biases],
        far_away(key_cache),
        far_away(value_cache),
    )


def project(core, gathered, weights, near, tp):
    sources, per, width = gathered.shape
    chips = sources // tp
    cores = len(weights)
    columns = weights[0].shape[1]

    def kernel(core_ref, a_ref, near_ref, *refs):
        far = refs[: cores - 1]
        out_ref, held, sems = refs[cores - 1], refs[cores : 2 * cores - 1], refs[-1]
        first = core_ref[0] == 0
        copies = []
        for t in range(tp):
            part = pl.ds(t * width, width)
            for c in range(cores - 1):
                copies.append(
                    pltpu.make_async_copy(far[c].at[part, :], held[c].at[part, :], sems.at[t])
                )
                copies[-1].start()
        lhs = [
            jnp.concatenate([a_ref[slot_of(n, t, near, tp)] for n in range(chips)], axis=0)
            for t in range(tp)
        ]
        accs = []
        for c in range(cores):
            acc = None
            for t in range(tp):
                source = near_ref
                if c:
                    copies[t].wait()
                    source = held[c - 1]
                part = jnp.dot(
                    lhs[t], source[t * width : (t + 1) * width, :], preferred_element_type=f32
                )
                acc = part if acc is None else acc + part
            accs.append(acc)
        if cores == 2:
            accs = [jnp.where(first, accs[0], accs[1]), jnp.where(first, accs[1], accs[0])]
        acc = jnp.concatenate(accs, axis=1).astype(bf16)
        for n in range(chips):
            for t in range(tp):
                out_ref[slot_of(n, t, near, tp)] = acc[n * per : (n + 1) * per]

    return pl.pallas_call(
        kernel,
        out_shape=pltpu.VMEM((sources, per, cores * columns), bf16),
        in_specs=[scalars, whole, whole] + [distant] * (cores - 1),
        out_specs=whole,
        scratch_shapes=[pltpu.VMEM(w.shape, w.dtype) for w in weights[1:]]
        + [pltpu.SemaphoreType.DMA((tp,))],
        compiler_params=params(8),
        cost_estimate=pl.CostEstimate(
            flops=2 * chips * per * tp * width * cores * columns,
            bytes_accessed=2 * tp * width * cores * columns,
            transcendentals=0,
        ),
        name="project",
    )(core, gathered, *weights)


def finish(finished, arrived, hidden_tiles, shape, cores, near, tp):
    sources, lines, wide = arrived.shape
    step_count, row_count, model_width = shape
    chips = sources // tp
    width = wide // cores

    def kernel(finished_ref, a_ref, h_ref, out_ref, y_scr):
        line = lax.broadcasted_iota(jnp.int32, (lines, 128), 0)
        done = jnp.zeros((lines, 128), jnp.int32)
        for r in range(row_count):
            done = jnp.where(line // step_count == r, finished_ref[r], done)
        for n, t, c in itertools.product(range(chips), range(tp), range(cores)):
            for b in range(width // 128):
                tile = ((n * cores + c) * tp + t) * (width // 128) + b
                start = c * width + b * 128
                moved = a_ref[slot_of(n, t, near, tp), :, start : start + 128].astype(f32)
                hidden = h_ref[tile]
                y_scr[tile] = jnp.where(done != 0, hidden, hidden + moved)
        for s in range(step_count):
            for b in range(model_width // 128):
                out_ref[s, :, b * 128 : (b + 1) * 128] = y_scr[
                    b, pl.ds(s, row_count, stride=step_count), :
                ].astype(bf16)

    return pl.pallas_call(
        kernel,
        out_shape=jax.ShapeDtypeStruct(shape, bf16),
        in_specs=[scalars, whole, whole],
        out_specs=whole,
        scratch_shapes=[pltpu.VMEM(hidden_tiles.shape, f32)],
        compiler_params=params(4),
        name="finish",
    )(finished, arrived, hidden_tiles)


def shards(
    hidden_in,
    norm_gain,
    w_query,
    key_weight_matrix,
    value_weight_matrix,
    bias_query,
    key_bias_vector,
    value_bias_vector,
    w_out,
    key_cache,
    value_cache,
    lengths,
    finished,
):
    step_count, row_count, model_width = hidden_in.shape
    lines = step_count * row_count
    head_dim = key_cache.shape[3]
    near = lax.axis_size("near")
    chips = lax.axis_size("far") * near
    chip_axes = ("far", "near")
    chip = lax.axis_index(chip_axes)
    cores = lax.axis_size("core")
    tp = lax.axis_size("tp")
    core = lax.axis_index("core")
    tp_index = lax.axis_index("tp")
    width = model_width // (chips * cores * tp)
    plane = ("far", "tp", "near")
    swap = [(i, cores - 1 - i) for i in range(cores)]

    def both(weight):
        return [weight] + ([lax.ppermute(weight, "core", swap)] if cores == 2 else [])

    queries_w = both(w_query)
    keys_w = both(key_weight_matrix)
    values_w = both(value_weight_matrix)

    core_place = core.astype(jnp.int32).reshape(1)
    tp_place = tp_index.astype(jnp.int32).reshape(1)
    chip_place = chip.astype(jnp.int32).reshape(1)
    if width % 128 == 0:
        *mine, scale, hidden_tiles = prepare(
            core_place, tp_place, chip_place, hidden_in, norm_gain, chips, cores, tp
        )
    else:
        by_row = jnp.transpose(hidden_in, (1, 0, 2)).reshape(lines, model_width).astype(f32)
        blocked = (by_row * norm_gain.astype(f32)).astype(bf16)
        blocked = blocked.reshape(lines, chips, cores, tp, width)
        mine = lax.dynamic_index_in_dim(blocked, tp_index, 3, keepdims=False)
        if cores == 2:
            mine = jnp.where(core == 0, mine, mine[:, :, ::-1])
        mine = jnp.transpose(mine, (1, 2, 0, 3)).reshape(chips, cores * lines, width)
        mine = [
            lax.dynamic_index_in_dim(mine, other_chip(chip, m, chips), 0, keepdims=False)
            for m in range(chips)
        ]
        scale = lax.rsqrt(jnp.mean(by_row * by_row, axis=-1, keepdims=True) + norm_eps)
        scale = jnp.broadcast_to(scale, (lines, 128))
    columns = []
    for m in range(chips):
        pairs = [(i, other_chip(i, m, chips)) for i in range(chips)]
        still = all(i == j for i, j in pairs)
        columns.append(mine[m] if still else lax.ppermute(mine[m], chip_axes, pairs))
    held = staged((w_query, key_weight_matrix, value_weight_matrix), mine[0])
    weights = [held] + list(zip(queries_w, keys_w, values_w))[1:]
    partials = qkv_partials(chip_place, columns, weights, near, tp)
    late_out, partials = lax.optimization_barrier((w_out, partials))
    outs_w = both(late_out)
    parts = lax.all_to_all(partials, plane, split_axis=0, concat_axis=0, tiled=True)
    block = min(key_cache.shape[2], 4096)
    attended = attention(
        lengths,
        finished,
        parts,
        scale,
        (bias_query, key_bias_vector, value_bias_vector),
        key_cache,
        value_cache,
        chips * tp,
        block,
    )
    gathered = lax.all_to_all(attended, plane, split_axis=0, concat_axis=0, tiled=True)
    product = project(core_place, gathered, outs_w, near, tp)
    arrived = lax.all_to_all(product, plane, split_axis=0, concat_axis=0, tiled=True)
    if width % 128 == 0:
        return finish(finished, arrived, hidden_tiles, hidden_in.shape, cores, near, tp)
    arrived = arrived.reshape(chips // near, tp, near, row_count, step_count, cores, width)
    projected = jnp.transpose(arrived, (4, 3, 0, 2, 5, 1, 6)).reshape(
        step_count, row_count, model_width
    )
    hidden = hidden_in.astype(f32)
    layer_out = jnp.where(finished[None, :, None] != 0, hidden, hidden + projected.astype(f32))
    return layer_out.astype(bf16)


def solution(mesh):
    gen = mesh.shape["gen"]
    cores = 2 if gen % 2 == 0 else 1
    chips = gen // cores
    near = 2 if chips % 2 == 0 else 1
    split = Mesh(
        mesh.devices.reshape(chips // near, near, cores, mesh.shape["tp"]),
        ("far", "near", "core", "tp"),
    )
    rows = ("far", "near", "core")
    every = rows + ("tp",)
    placed = (
        P(None, rows, None),
        P(),
        P(every, None),
        P(every, None),
        P(every, None),
        P("tp"),
        P("tp"),
        P("tp"),
        P(None, every),
        P(rows, "tp", None, None),
        P(rows, "tp", None, None),
        P(rows),
        P(rows),
    )
    return jax.shard_map(
        shards, mesh=split, in_specs=placed, out_specs=P(None, rows, None), check_vma=False
    )
```

```python
import itertools
import math

import jax
import jax.numpy as jnp
from jax import lax
from jax.experimental import pallas as pl
from jax.experimental.pallas import tpu as pltpu
from jax.sharding import Mesh
from jax.sharding import PartitionSpec as P

norm_eps = 1e-06
rope_base = 1000000.0
masked_score = -1e30
bf16 = jnp.bfloat16
f32 = jnp.float32


whole = pl.BlockSpec(memory_space=pltpu.VMEM)
scalars = pl.BlockSpec(memory_space=pltpu.SMEM)
distant = pl.BlockSpec(memory_space=pltpu.HBM)


def far_away(array):
    return pltpu.with_memory_space_constraint(array, pltpu.HBM)


def params(mib):
    return pltpu.CompilerParams(vmem_limit_bytes=mib << 20)


def other_chip(chip, m, chips):
    if chips & (chips - 1) == 0:
        return chip ^ m
    return (m - chip) % chips


def slot_of(n, t, near, tp):
    return ((n // near) * tp + t) * near + n % near


def prepare(core, tp_index, chip, hidden_in, norm_gain, w_query, chips, cores, tp):
    step_count, row_count, model_width = hidden_in.shape
    lines = step_count * row_count
    width = model_width // (chips * cores * tp)

    def kernel(core_ref, tp_ref, chip_ref, h_hbm, g_hbm, w_hbm, *refs):
        mine_refs, scale_ref, x_ref, w_ref = refs[:chips], *refs[chips : chips + 3]
        h_ref, g_ref, g_scr, sems = refs[chips + 3 :]
        copies = [
            pltpu.make_async_copy(h_hbm, h_ref, sems.at[0]),
            pltpu.make_async_copy(g_hbm, g_ref, sems.at[1]),
            pltpu.make_async_copy(w_hbm, w_ref, sems.at[2]),
        ]
        for copy in copies:
            copy.start()
        for copy in copies[:2]:
            copy.wait()
        for s in range(step_count):
            for b in range(model_width // 128):
                x_ref[b, pl.ds(s, row_count, stride=step_count), :] = h_ref[
                    s, :, b * 128 : (b + 1) * 128
                ].astype(f32)
        g_scr[...] = g_ref[...].astype(f32)
        own = core_ref[0]
        for m in range(chips):
            n = other_chip(chip_ref[0], m, chips)
            for c in range(cores):
                at = own if c == 0 else 1 - own
                block = ((n * cores + at) * tp + tp_ref[0]) * (width // 128)
                for b in range(width // 128):
                    x = x_ref[block + b] * g_scr[pl.ds(block + b, 1), :]
                    mine_refs[m][c * lines : (c + 1) * lines, b * 128 : (b + 1) * 128] = x.astype(
                        bf16
                    )
        square = jnp.zeros((lines, 128), f32)
        for b in range(model_width // 128):
            square = square + x_ref[b] * x_ref[b]
        mean = jnp.sum(square, axis=1, keepdims=True) * (1.0 / model_width)
        scale_ref[...] = jnp.broadcast_to(lax.rsqrt(mean + norm_eps), (lines, 128))
        copies[2].wait()

    return pl.pallas_call(
        kernel,
        out_shape=(jax.ShapeDtypeStruct((cores * lines, width), bf16),) * chips
        + (
            jax.ShapeDtypeStruct((lines, 128), f32),
            pltpu.VMEM((model_width // 128, lines, 128), f32),
            pltpu.VMEM(w_query.shape, bf16),
        ),
        in_specs=[scalars, scalars, scalars, distant, distant, distant],
        out_specs=(whole,) * (chips + 3),
        scratch_shapes=[
            pltpu.VMEM(hidden_in.shape, bf16),
            pltpu.VMEM((model_width // 128, 128), bf16),
            pltpu.VMEM((model_width // 128, 128), f32),
            pltpu.SemaphoreType.DMA((3,)),
        ],
        compiler_params=params(4),
        name="prepare",
    )(
        core,
        tp_index,
        chip,
        far_away(hidden_in),
        far_away(norm_gain.reshape(model_width // 128, 128)),
        far_away(w_query),
    )


def staged(arrays, after):
    count = len(arrays)

    def kernel(*refs):
        sources, outs, sems = refs[:count], refs[count + 1 : 2 * count + 1], refs[-1]
        copies = [pltpu.make_async_copy(sources[i], outs[i], sems.at[i]) for i in range(count)]
        for copy in copies:
            copy.start()
        for copy in copies:
            copy.wait()

    return pl.pallas_call(
        kernel,
        out_shape=tuple(pltpu.VMEM(a.shape, a.dtype) for a in arrays),
        in_specs=[distant] * count + [pl.BlockSpec(memory_space=pl.ANY)],
        out_specs=(whole,) * count,
        scratch_shapes=[pltpu.SemaphoreType.DMA((count,))],
        compiler_params=params(1),
        cost_estimate=pl.CostEstimate(
            flops=0, bytes_accessed=sum(math.prod(a.shape) * 2 for a in arrays), transcendentals=0
        ),
        name="stage_weights",
    )(*[far_away(a) for a in arrays], after)


def qkv_partials(chip, columns, weights, near, tp, later):
    chips = len(columns)
    depth, width = columns[0].shape
    cores = len(weights)
    per = depth // cores
    rows = chips * per
    sizes = [w.shape[1] // tp for w in weights[0]]
    total = sum(sizes)
    flat = [w for group in weights for w in group]

    def kernel(chip_ref, *refs):
        x_refs, w_refs, out_ref = refs[:chips], refs[chips : chips + len(flat)], refs[-1]
        lhs = [
            jnp.concatenate([x[c * per : (c + 1) * per] for x in x_refs], axis=0)
            for c in range(cores)
        ]
        places = [other_chip(chip_ref[0], m, chips) for m in range(chips)]
        for t in range(tp):
            slots = [slot_of(n, t, near, tp) for n in places]
            start = 0
            for kind, size in enumerate(sizes):
                acc = None
                for c in range(cores):
                    w = w_refs[c * 3 + kind][:, t * size : (t + 1) * size]
                    part = jnp.dot(lhs[c], w, preferred_element_type=f32)
                    acc = part if acc is None else acc + part
                acc = acc.astype(bf16)
                for m in range(chips):
                    out_ref[slots[m], :, start : start + size] = acc[m * per : (m + 1) * per]
                start += size

    return pl.pallas_call(
        kernel,
        out_shape=pltpu.VMEM((chips * tp, per, total), bf16),
        in_specs=[scalars] + [whole] * (chips + len(flat)) + [distant] * len(later),
        out_specs=whole,
        compiler_params=params(6),
        cost_estimate=pl.CostEstimate(
            flops=2 * cores * rows * width * total * tp,
            bytes_accessed=2 * cores * width * total * tp,
            transcendentals=0,
        ),
        name="qkv_partials",
    )(chip, *columns, *flat, *[far_away(x) for x in later])


def attention(lengths, finished, parts, scale, biases, key_cache, value_cache, copies, block):
    sources, lines, total = parts.shape
    row_count, kv_heads, cache_len, head_dim = key_cache.shape
    steps = lines // row_count
    kv_width = kv_heads * head_dim
    q_width = total - 2 * kv_width
    heads = q_width // head_dim
    group = heads // kv_heads
    queries = group * steps
    fresh = 8
    small = min(block, 1024)
    factor = math.log2(math.e) / math.sqrt(head_dim)
    pairs = [(r, j) for r in range(row_count) for j in range(kv_heads)]

    def kernel(length_ref, finished_ref, p_ref, scale_ref, bq_ref, bk_ref, bv_ref, k_ref, v_ref,
               out_ref, q_scr, kn_scr, vn_scr, s_scr, o_scr):
        lives = [
            jnp.where(finished_ref[r] != 0, 0, length_ref[r]) for r in range(row_count)
        ]
        larges = [length // block for length in lives]
        smalls = [
            (length - large * block + small - 1) // small for length, large in zip(lives, larges)
        ]
        tails = [large * block for large in larges]

        def large_at(r, i):
            return pl.multiple_of(i * block, block)

        def small_at(r, i):
            return pl.multiple_of(tails[r] + i * small, small)

        scale = scale_ref[...]
        line = lax.broadcasted_iota(jnp.int32, (lines, head_dim), 0)
        lane = lax.broadcasted_iota(jnp.int32, (lines, head_dim), 1)
        position = line % steps
        for r in range(row_count):
            position = position + jnp.where(line // steps == r, length_ref[r], 0)
        half = head_dim // 2
        pair = (lane % half).astype(f32)
        frequency = jnp.exp(pair * (-2.0 * math.log(rope_base) / head_dim))
        angles = position.astype(f32) * frequency
        cos = jnp.cos(angles)
        sin = jnp.where(lane < half, -1.0, 1.0) * jnp.sin(angles)

        def summed(start, bias_row):
            terms = [p_ref[i, :, start : start + head_dim].astype(f32) for i in range(sources)]
            while len(terms) > 1:
                terms = [sum(terms[i : i + 2]) for i in range(0, len(terms), 2)]
            return terms[0] * scale + bias_row.astype(f32)

        def rotated(start, bias_row):
            head = summed(start, bias_row)
            return head * cos + pltpu.roll(head, half, 1) * sin

        kn_scr[...] = jnp.zeros_like(kn_scr)
        vn_scr[...] = jnp.zeros_like(vn_scr)
        for h in range(heads):
            q = rotated(h * head_dim, bq_ref[h : h + 1, :])
            for r in range(row_count):
                g = h % group
                q_scr[r, h // group, g * steps : (g + 1) * steps, :] = q[r * steps : (r + 1) * steps]
        for j in range(kv_heads):
            k = rotated(q_width + j * head_dim, bk_ref[j : j + 1, :])
            v = summed(q_width + kv_width + j * head_dim, bv_ref[j : j + 1, :])
            for r in range(row_count):
                kn_scr[r, j, 0:steps, :] = k[r * steps : (r + 1) * steps]
                vn_scr[r, j, 0:steps, :] = v[r * steps : (r + 1) * steps]
        step_of = lax.broadcasted_iota(jnp.int32, (queries, fresh), 0) % steps
        allowed = lax.broadcasted_iota(jnp.int32, (queries, fresh), 1) <= step_of
        nt = (((1,), (1,)), ((), ()))
        qs = {}
        new_scores = {}
        new_tops = {}
        for r, j in pairs:
            qs[r, j] = q_scr[r, j].astype(bf16)
            s = lax.dot_general(
                qs[r, j], kn_scr[r, j].astype(bf16), nt, preferred_element_type=f32
            )
            new_scores[r, j] = jnp.where(allowed, s, masked_score)
            new_tops[r, j] = jnp.max(new_scores[r, j], axis=1, keepdims=True)
        tops = {}
        lane_sums = {}
        totals = {}
        for r in range(row_count):

            def scores(start, size, masked, most):
                out = []
                for j in range(kv_heads):
                    s = lax.dot_general(
                        qs[r, j], k_ref[r, j, pl.ds(start, size), :], nt, preferred_element_type=f32
                    )
                    if masked:
                        place = start + lax.broadcasted_iota(jnp.int32, (queries, size), 1)
                        s = jnp.where(place < lives[r], s, masked_score)
                    s_scr[j, :, pl.ds(start, size)] = s
                    top = most[j]
                    for b in range(size // 128):
                        top = jnp.maximum(top, s[:, b * 128 : (b + 1) * 128])
                    out.append(top)
                return tuple(out)

            def score_large(i, most):
                start = large_at(r, i)
                return scores(start, block, False, most)

            def score_small(i, most):
                start = small_at(r, i)
                return scores(start, small, True, most)

            most = tuple(jnp.full((queries, 128), masked_score, f32) for _ in range(kv_heads))
            most = lax.fori_loop(0, larges[r], score_large, most)
            most = lax.fori_loop(0, smalls[r], score_small, most)
            for j in range(kv_heads):
                tops[r, j] = jnp.maximum(
                    jnp.max(most[j], axis=1, keepdims=True), new_tops[r, j]
                )

            def gather(start, size, carry):
                lanes, accs = carry
                new_lanes = []
                new_accs = []
                for j in range(kv_heads):
                    p = jnp.exp2((s_scr[j, :, pl.ds(start, size)] - tops[r, j]) * factor)
                    lane_sum = lanes[j]
                    for b in range(size // 128):
                        lane_sum = lane_sum + p[:, b * 128 : (b + 1) * 128]
                    new_lanes.append(lane_sum)
                    new_accs.append(
                        accs[j]
                        + jnp.dot(
                            p.astype(bf16),
                            v_ref[r, j, pl.ds(start, size), :],
                            preferred_element_type=f32,
                        )
                    )
                return tuple(new_lanes), tuple(new_accs)

            def gather_large(i, carry):
                start = large_at(r, i)
                return gather(start, block, carry)

            def gather_small(i, carry):
                start = small_at(r, i)
                return gather(start, small, carry)

            carry = (
                tuple(jnp.zeros((queries, 128), f32) for _ in range(kv_heads)),
                tuple(jnp.zeros((queries, head_dim), f32) for _ in range(kv_heads)),
            )
            carry = lax.fori_loop(0, larges[r], gather_large, carry)
            carry = lax.fori_loop(0, smalls[r], gather_small, carry)
            for j in range(kv_heads):
                lane_sums[r, j] = carry[0][j]
                totals[r, j] = carry[1][j]
        for r, j in pairs:
            p = jnp.exp2((new_scores[r, j] - tops[r, j]) * factor)
            total_sum = jnp.sum(lane_sums[r, j], axis=1, keepdims=True) + jnp.sum(
                p, axis=1, keepdims=True
            )
            o = totals[r, j] + jnp.dot(
                p.astype(bf16), vn_scr[r, j].astype(bf16), preferred_element_type=f32
            )
            o = o / total_sum
            for g in range(group):
                col = (j * group + g) * head_dim
                o_scr[r * steps : (r + 1) * steps, col : col + head_dim] = o[
                    g * steps : (g + 1) * steps
                ]
        result = o_scr[...].astype(bf16)
        for n in range(copies):
            out_ref[n] = result

    flops = 4 * row_count * kv_heads * queries * cache_len * head_dim
    return pl.pallas_call(
        kernel,
        out_shape=pltpu.VMEM((copies, lines, q_width), bf16),
        in_specs=[scalars, scalars] + [whole] * 7,
        out_specs=whole,
        scratch_shapes=[
            pltpu.VMEM((row_count, kv_heads, queries, head_dim), f32),
            pltpu.VMEM((row_count, kv_heads, fresh, head_dim), f32),
            pltpu.VMEM((row_count, kv_heads, fresh, head_dim), f32),
            pltpu.VMEM((kv_heads, queries, cache_len), f32),
            pltpu.VMEM((lines, q_width), f32),
        ],
        compiler_params=params(6),
        cost_estimate=pl.CostEstimate(
            flops=flops,
            bytes_accessed=4 * row_count * kv_heads * cache_len * head_dim,
            transcendentals=0,
        ),
        name="attention",
    )(
        lengths,
        finished,
        parts,
        scale,
        *[b.reshape(-1, head_dim) for b in biases],
        key_cache,
        value_cache,
    )


def project(core, gathered, weights, near, tp):
    sources, per, width = gathered.shape
    chips = sources // tp
    cores = len(weights)
    columns = weights[0].shape[1]

    def kernel(core_ref, a_ref, near_ref, *refs):
        far = refs[: cores - 1]
        out_ref, held, sems = refs[cores - 1], refs[cores : 2 * cores - 1], refs[-1]
        first = core_ref[0] == 0
        copies = []
        for t in range(tp):
            part = pl.ds(t * width, width)
            for c in range(cores - 1):
                copies.append(
                    pltpu.make_async_copy(far[c].at[part, :], held[c].at[part, :], sems.at[t])
                )
                copies[-1].start()
        lhs = [
            jnp.concatenate([a_ref[slot_of(n, t, near, tp)] for n in range(chips)], axis=0)
            for t in range(tp)
        ]
        accs = []
        for c in range(cores):
            acc = None
            for t in range(tp):
                source = near_ref
                if c:
                    copies[t].wait()
                    source = held[c - 1]
                part = jnp.dot(
                    lhs[t], source[t * width : (t + 1) * width, :], preferred_element_type=f32
                )
                acc = part if acc is None else acc + part
            accs.append(acc)
        if cores == 2:
            accs = [jnp.where(first, accs[0], accs[1]), jnp.where(first, accs[1], accs[0])]
        acc = jnp.concatenate(accs, axis=1).astype(bf16)
        for n in range(chips):
            for t in range(tp):
                out_ref[slot_of(n, t, near, tp)] = acc[n * per : (n + 1) * per]

    return pl.pallas_call(
        kernel,
        out_shape=pltpu.VMEM((sources, per, cores * columns), bf16),
        in_specs=[scalars, whole, whole] + [distant] * (cores - 1),
        out_specs=whole,
        scratch_shapes=[pltpu.VMEM(w.shape, w.dtype) for w in weights[1:]]
        + [pltpu.SemaphoreType.DMA((tp,))],
        compiler_params=params(8),
        cost_estimate=pl.CostEstimate(
            flops=2 * chips * per * tp * width * cores * columns,
            bytes_accessed=2 * tp * width * cores * columns,
            transcendentals=0,
        ),
        name="project",
    )(core, gathered, *weights)


def finish(finished, arrived, hidden_tiles, shape, cores, near, tp):
    sources, lines, wide = arrived.shape
    step_count, row_count, model_width = shape
    chips = sources // tp
    width = wide // cores

    def kernel(finished_ref, a_ref, h_ref, out_ref, y_scr, out_scr, sems):
        line = lax.broadcasted_iota(jnp.int32, (lines, 128), 0)
        done = jnp.zeros((lines, 128), jnp.int32)
        for r in range(row_count):
            done = jnp.where(line // step_count == r, finished_ref[r], done)
        copies = []
        span = cores * tp * width
        for n in range(chips):
            for c, t in itertools.product(range(cores), range(tp)):
                for b in range(width // 128):
                    tile = ((n * cores + c) * tp + t) * (width // 128) + b
                    start = c * width + b * 128
                    moved = a_ref[slot_of(n, t, near, tp), :, start : start + 128].astype(f32)
                    hidden = h_ref[tile]
                    y_scr[tile] = jnp.where(done != 0, hidden, hidden + moved)
            for s in range(step_count):
                for b in range(n * span // 128, (n + 1) * span // 128):
                    out_scr[s, :, b * 128 : (b + 1) * 128] = y_scr[
                        b, pl.ds(s, row_count, stride=step_count), :
                    ].astype(bf16)
            part = pl.ds(n * span, span)
            copies.append(
                pltpu.make_async_copy(
                    out_scr.at[:, :, part], out_ref.at[:, :, part], sems.at[n]
                )
            )
            copies[-1].start()
        for copy in copies:
            copy.wait()

    return pl.pallas_call(
        kernel,
        out_shape=jax.ShapeDtypeStruct(shape, bf16),
        in_specs=[scalars, whole, whole],
        out_specs=distant,
        scratch_shapes=[
            pltpu.VMEM(hidden_tiles.shape, f32),
            pltpu.VMEM(shape, bf16),
            pltpu.SemaphoreType.DMA((chips,)),
        ],
        compiler_params=params(4),
        name="finish",
    )(finished, arrived, hidden_tiles)


def shards(
    hidden_in,
    norm_gain,
    w_query,
    key_weight_matrix,
    value_weight_matrix,
    bias_query,
    key_bias_vector,
    value_bias_vector,
    w_out,
    key_cache,
    value_cache,
    lengths,
    finished,
):
    step_count, row_count, model_width = hidden_in.shape
    lines = step_count * row_count
    head_dim = key_cache.shape[3]
    near = lax.axis_size("near")
    chips = lax.axis_size("far") * near
    chip_axes = ("far", "near")
    chip = lax.axis_index(chip_axes)
    cores = lax.axis_size("core")
    tp = lax.axis_size("tp")
    core = lax.axis_index("core")
    tp_index = lax.axis_index("tp")
    width = model_width // (chips * cores * tp)
    plane = ("far", "tp", "near")
    swap = [(i, cores - 1 - i) for i in range(cores)]

    def both(weight):
        return [weight] + ([lax.ppermute(weight, "core", swap)] if cores == 2 else [])

    queries_w = both(w_query)
    keys_w = both(key_weight_matrix)
    values_w = both(value_weight_matrix)

    core_place = core.astype(jnp.int32).reshape(1)
    tp_place = tp_index.astype(jnp.int32).reshape(1)
    chip_place = chip.astype(jnp.int32).reshape(1)
    if width % 128 == 0:
        *mine, scale, hidden_tiles, held_query = prepare(
            core_place, tp_place, chip_place, hidden_in, norm_gain, w_query, chips, cores, tp
        )
    else:
        by_row = jnp.transpose(hidden_in, (1, 0, 2)).reshape(lines, model_width).astype(f32)
        blocked = (by_row * norm_gain.astype(f32)).astype(bf16)
        blocked = blocked.reshape(lines, chips, cores, tp, width)
        mine = lax.dynamic_index_in_dim(blocked, tp_index, 3, keepdims=False)
        if cores == 2:
            mine = jnp.where(core == 0, mine, mine[:, :, ::-1])
        mine = jnp.transpose(mine, (1, 2, 0, 3)).reshape(chips, cores * lines, width)
        mine = [
            lax.dynamic_index_in_dim(mine, other_chip(chip, m, chips), 0, keepdims=False)
            for m in range(chips)
        ]
        scale = lax.rsqrt(jnp.mean(by_row * by_row, axis=-1, keepdims=True) + norm_eps)
        scale = jnp.broadcast_to(scale, (lines, 128))
    columns = []
    for m in range(chips):
        pairs = [(i, other_chip(i, m, chips)) for i in range(chips)]
        still = all(i == j for i, j in pairs)
        columns.append(mine[m] if still else lax.ppermute(mine[m], chip_axes, pairs))
    if width % 128 == 0:
        held = (held_query,) + tuple(staged((key_weight_matrix, value_weight_matrix), mine[0]))
    else:
        held = staged((w_query, key_weight_matrix, value_weight_matrix), mine[0])
    weights = [held] + list(zip(queries_w, keys_w, values_w))[1:]
    partials = qkv_partials(chip_place, columns, weights, near, tp, (key_cache, value_cache))
    parts = lax.all_to_all(partials, plane, split_axis=0, concat_axis=0, tiled=True)
    late_out, parts = lax.optimization_barrier((w_out, parts))
    outs_w = both(late_out)
    block = min(key_cache.shape[2], 4096)
    attended = attention(
        lengths,
        finished,
        parts,
        scale,
        (bias_query, key_bias_vector, value_bias_vector),
        key_cache,
        value_cache,
        chips * tp,
        block,
    )
    gathered = lax.all_to_all(attended, plane, split_axis=0, concat_axis=0, tiled=True)
    product = project(core_place, gathered, outs_w, near, tp)
    arrived = lax.all_to_all(product, plane, split_axis=0, concat_axis=0, tiled=True)
    if width % 128 == 0:
        return finish(finished, arrived, hidden_tiles, hidden_in.shape, cores, near, tp)
    arrived = arrived.reshape(chips // near, tp, near, row_count, step_count, cores, width)
    projected = jnp.transpose(arrived, (4, 3, 0, 2, 5, 1, 6)).reshape(
        step_count, row_count, model_width
    )
    hidden = hidden_in.astype(f32)
    layer_out = jnp.where(finished[None, :, None] != 0, hidden, hidden + projected.astype(f32))
    return layer_out.astype(bf16)


def solution(mesh):
    gen = mesh.shape["gen"]
    cores = 2 if gen % 2 == 0 else 1
    chips = gen // cores
    near = 2 if chips % 2 == 0 else 1
    split = Mesh(
        mesh.devices.reshape(chips // near, near, cores, mesh.shape["tp"]),
        ("far", "near", "core", "tp"),
    )
    rows = ("far", "near", "core")
    every = rows + ("tp",)
    placed = (
        P(None, rows, None),
        P(),
        P(every, None),
        P(every, None),
        P(every, None),
        P("tp"),
        P("tp"),
        P("tp"),
        P(None, every),
        P(rows, "tp", None, None),
        P(rows, "tp", None, None),
        P(rows),
        P(rows),
    )
    return jax.shard_map(
        shards, mesh=split, in_specs=placed, out_specs=P(None, rows, None), check_vma=False
    )
```

```python
import itertools
import math

import jax
import jax.numpy as jnp
from jax import lax
from jax.experimental import pallas as pl
from jax.experimental.pallas import tpu as pltpu
from jax.sharding import Mesh
from jax.sharding import PartitionSpec as P

norm_eps = 1e-06
rope_base = 1000000.0
masked_score = -1e30
bf16 = jnp.bfloat16
f32 = jnp.float32


whole = pl.BlockSpec(memory_space=pltpu.VMEM)
scalars = pl.BlockSpec(memory_space=pltpu.SMEM)
distant = pl.BlockSpec(memory_space=pltpu.HBM)


def far_away(array):
    return pltpu.with_memory_space_constraint(array, pltpu.HBM)


def params(mib):
    return pltpu.CompilerParams(vmem_limit_bytes=mib << 20)


def other_chip(chip, m, chips):
    if chips & (chips - 1) == 0:
        return chip ^ m
    return (m - chip) % chips


def slot_of(n, t, near, tp):
    return ((n // near) * tp + t) * near + n % near


def prepare(core, tp_index, chip, hidden_in, norm_gain, w_query, chips, cores, tp):
    step_count, row_count, model_width = hidden_in.shape
    lines = step_count * row_count
    width = model_width // (chips * cores * tp)

    def kernel(core_ref, tp_ref, chip_ref, h_hbm, g_hbm, w_hbm, *refs):
        mine_refs, scale_ref, x_ref, w_ref = refs[:chips], *refs[chips : chips + 3]
        h_ref, g_ref, g_scr, sems = refs[chips + 3 :]
        copies = [
            pltpu.make_async_copy(h_hbm, h_ref, sems.at[0]),
            pltpu.make_async_copy(g_hbm, g_ref, sems.at[1]),
            pltpu.make_async_copy(w_hbm, w_ref, sems.at[2]),
        ]
        for copy in copies:
            copy.start()
        for copy in copies[:2]:
            copy.wait()
        for s in range(step_count):
            for b in range(model_width // 128):
                x_ref[b, pl.ds(s, row_count, stride=step_count), :] = h_ref[
                    s, :, b * 128 : (b + 1) * 128
                ].astype(f32)
        g_scr[...] = g_ref[...].astype(f32)
        own = core_ref[0]
        for m in range(chips):
            n = other_chip(chip_ref[0], m, chips)
            for c in range(cores):
                at = own if c == 0 else 1 - own
                block = ((n * cores + at) * tp + tp_ref[0]) * (width // 128)
                for b in range(width // 128):
                    x = x_ref[block + b] * g_scr[pl.ds(block + b, 1), :]
                    mine_refs[m][c * lines : (c + 1) * lines, b * 128 : (b + 1) * 128] = x.astype(
                        bf16
                    )
        square = jnp.zeros((lines, 128), f32)
        for b in range(model_width // 128):
            square = square + x_ref[b] * x_ref[b]
        mean = jnp.sum(square, axis=1, keepdims=True) * (1.0 / model_width)
        scale_ref[...] = jnp.broadcast_to(lax.rsqrt(mean + norm_eps), (lines, 128))
        copies[2].wait()

    return pl.pallas_call(
        kernel,
        out_shape=(jax.ShapeDtypeStruct((cores * lines, width), bf16),) * chips
        + (
            jax.ShapeDtypeStruct((lines, 128), f32),
            pltpu.VMEM((model_width // 128, lines, 128), f32),
            pltpu.VMEM(w_query.shape, bf16),
        ),
        in_specs=[scalars, scalars, scalars, distant, distant, distant],
        out_specs=(whole,) * (chips + 3),
        scratch_shapes=[
            pltpu.VMEM(hidden_in.shape, bf16),
            pltpu.VMEM((model_width // 128, 128), bf16),
            pltpu.VMEM((model_width // 128, 128), f32),
            pltpu.SemaphoreType.DMA((3,)),
        ],
        compiler_params=params(4),
        name="prepare",
    )(
        core,
        tp_index,
        chip,
        far_away(hidden_in),
        far_away(norm_gain.reshape(model_width // 128, 128)),
        far_away(w_query),
    )


def staged(arrays, after):
    count = len(arrays)

    def kernel(*refs):
        sources, outs, sems = refs[:count], refs[count + 1 : 2 * count + 1], refs[-1]
        copies = [pltpu.make_async_copy(sources[i], outs[i], sems.at[i]) for i in range(count)]
        for copy in copies:
            copy.start()
        for copy in copies:
            copy.wait()

    return pl.pallas_call(
        kernel,
        out_shape=tuple(pltpu.VMEM(a.shape, a.dtype) for a in arrays),
        in_specs=[distant] * count + [pl.BlockSpec(memory_space=pl.ANY)],
        out_specs=(whole,) * count,
        scratch_shapes=[pltpu.SemaphoreType.DMA((count,))],
        compiler_params=params(1),
        cost_estimate=pl.CostEstimate(
            flops=0, bytes_accessed=sum(math.prod(a.shape) * 2 for a in arrays), transcendentals=0
        ),
        name="stage_weights",
    )(*[far_away(a) for a in arrays], after)


def qkv_partials(chip, columns, weights, near, tp, later):
    chips = len(columns)
    depth, width = columns[0].shape
    cores = len(weights)
    per = depth // cores
    rows = chips * per
    sizes = [w.shape[1] // tp for w in weights[0]]
    total = sum(sizes)
    flat = [w for group in weights for w in group]

    def kernel(chip_ref, *refs):
        x_refs, w_refs, out_ref = refs[:chips], refs[chips : chips + len(flat)], refs[-1]
        lhs = [
            jnp.concatenate([x[c * per : (c + 1) * per] for x in x_refs], axis=0)
            for c in range(cores)
        ]
        places = [other_chip(chip_ref[0], m, chips) for m in range(chips)]
        for t in range(tp):
            slots = [slot_of(n, t, near, tp) for n in places]
            start = 0
            for kind, size in enumerate(sizes):
                acc = None
                for c in range(cores):
                    w = w_refs[c * 3 + kind][:, t * size : (t + 1) * size]
                    part = jnp.dot(lhs[c], w, preferred_element_type=f32)
                    acc = part if acc is None else acc + part
                acc = acc.astype(bf16)
                for m in range(chips):
                    out_ref[slots[m], :, start : start + size] = acc[m * per : (m + 1) * per]
                start += size

    return pl.pallas_call(
        kernel,
        out_shape=pltpu.VMEM((chips * tp, per, total), bf16),
        in_specs=[scalars] + [whole] * (chips + len(flat)) + [distant] * len(later),
        out_specs=whole,
        compiler_params=params(6),
        cost_estimate=pl.CostEstimate(
            flops=2 * cores * rows * width * total * tp,
            bytes_accessed=2 * cores * width * total * tp,
            transcendentals=0,
        ),
        name="qkv_partials",
    )(chip, *columns, *flat, *[far_away(x) for x in later])


def attention(lengths, finished, parts, scale, biases, key_cache, value_cache, copies, block):
    sources, lines, total = parts.shape
    row_count, kv_heads, cache_len, head_dim = key_cache.shape
    steps = lines // row_count
    kv_width = kv_heads * head_dim
    q_width = total - 2 * kv_width
    heads = q_width // head_dim
    group = heads // kv_heads
    queries = group * steps
    fresh = 8
    small = min(block, 1024)
    sizes = [block >> i for i in (0, 2) if block >> i > small]
    factor = math.log2(math.e) / math.sqrt(head_dim)
    pairs = [(r, j) for r in range(row_count) for j in range(kv_heads)]

    def kernel(length_ref, finished_ref, p_ref, scale_ref, bq_ref, bk_ref, bv_ref, k_ref, v_ref,
               out_ref, q_scr, kn_scr, vn_scr, s_scr, o_scr):
        lives = [
            jnp.where(finished_ref[r] != 0, 0, length_ref[r]) for r in range(row_count)
        ]
        plans = []
        for length in lives:
            offset = length * 0
            plan = []
            for size in sizes:
                count = (length - offset) // size
                plan.append((offset, count, size, False))
                offset = offset + count * size
            plan.append((offset, (length - offset + small - 1) // small, small, True))
            plans.append(plan)

        def over(plan, step, carry):
            for offset, count, size, masked in plan:

                def one(i, carry, offset=offset, size=size, masked=masked):
                    return step(pl.multiple_of(offset + i * size, small), size, masked, carry)

                carry = lax.fori_loop(0, count, one, carry)
            return carry

        scale = scale_ref[...]
        line = lax.broadcasted_iota(jnp.int32, (lines, head_dim), 0)
        lane = lax.broadcasted_iota(jnp.int32, (lines, head_dim), 1)
        position = line % steps
        for r in range(row_count):
            position = position + jnp.where(line // steps == r, length_ref[r], 0)
        half = head_dim // 2
        pair = (lane % half).astype(f32)
        frequency = jnp.exp(pair * (-2.0 * math.log(rope_base) / head_dim))
        angles = position.astype(f32) * frequency
        cos = jnp.cos(angles)
        sin = jnp.where(lane < half, -1.0, 1.0) * jnp.sin(angles)

        def summed(start, bias_row):
            terms = [p_ref[i, :, start : start + head_dim].astype(f32) for i in range(sources)]
            while len(terms) > 1:
                terms = [sum(terms[i : i + 2]) for i in range(0, len(terms), 2)]
            return terms[0] * scale + bias_row.astype(f32)

        def rotated(start, bias_row):
            head = summed(start, bias_row)
            return head * cos + pltpu.roll(head, half, 1) * sin

        kn_scr[...] = jnp.zeros_like(kn_scr)
        vn_scr[...] = jnp.zeros_like(vn_scr)
        for h in range(heads):
            q = rotated(h * head_dim, bq_ref[h : h + 1, :])
            for r in range(row_count):
                g = h % group
                q_scr[r, h // group, g * steps : (g + 1) * steps, :] = q[r * steps : (r + 1) * steps]
        for j in range(kv_heads):
            k = rotated(q_width + j * head_dim, bk_ref[j : j + 1, :])
            v = summed(q_width + kv_width + j * head_dim, bv_ref[j : j + 1, :])
            for r in range(row_count):
                kn_scr[r, j, 0:steps, :] = k[r * steps : (r + 1) * steps]
                vn_scr[r, j, 0:steps, :] = v[r * steps : (r + 1) * steps]
        step_of = lax.broadcasted_iota(jnp.int32, (queries, fresh), 0) % steps
        allowed = lax.broadcasted_iota(jnp.int32, (queries, fresh), 1) <= step_of
        nt = (((1,), (1,)), ((), ()))
        qs = {}
        new_scores = {}
        new_tops = {}
        for r, j in pairs:
            qs[r, j] = q_scr[r, j].astype(bf16)
            s = lax.dot_general(
                qs[r, j], kn_scr[r, j].astype(bf16), nt, preferred_element_type=f32
            )
            new_scores[r, j] = jnp.where(allowed, s, masked_score)
            new_tops[r, j] = jnp.max(new_scores[r, j], axis=1, keepdims=True)
        tops = {}
        lane_sums = {}
        totals = {}
        for r in range(row_count):

            def scores(start, size, masked, most):
                out = []
                for j in range(kv_heads):
                    s = lax.dot_general(
                        qs[r, j], k_ref[r, j, pl.ds(start, size), :], nt, preferred_element_type=f32
                    )
                    if masked:
                        place = start + lax.broadcasted_iota(jnp.int32, (queries, size), 1)
                        s = jnp.where(place < lives[r], s, masked_score)
                    s_scr[j, :, pl.ds(start, size)] = s
                    top = most[j]
                    for b in range(size // 128):
                        top = jnp.maximum(top, s[:, b * 128 : (b + 1) * 128])
                    out.append(top)
                return tuple(out)

            most = tuple(jnp.full((queries, 128), masked_score, f32) for _ in range(kv_heads))
            most = over(plans[r], scores, most)
            for j in range(kv_heads):
                tops[r, j] = jnp.maximum(
                    jnp.max(most[j], axis=1, keepdims=True), new_tops[r, j]
                )

            def gather(start, size, masked, carry):
                lanes, accs = carry
                new_lanes = []
                new_accs = []
                for j in range(kv_heads):
                    p = jnp.exp2((s_scr[j, :, pl.ds(start, size)] - tops[r, j]) * factor)
                    lane_sum = lanes[j]
                    for b in range(size // 128):
                        lane_sum = lane_sum + p[:, b * 128 : (b + 1) * 128]
                    new_lanes.append(lane_sum)
                    new_accs.append(
                        accs[j]
                        + jnp.dot(
                            p.astype(bf16),
                            v_ref[r, j, pl.ds(start, size), :],
                            preferred_element_type=f32,
                        )
                    )
                return tuple(new_lanes), tuple(new_accs)

            carry = (
                tuple(jnp.zeros((queries, 128), f32) for _ in range(kv_heads)),
                tuple(jnp.zeros((queries, head_dim), f32) for _ in range(kv_heads)),
            )
            carry = over(plans[r], gather, carry)
            for j in range(kv_heads):
                lane_sums[r, j] = carry[0][j]
                totals[r, j] = carry[1][j]
        for r, j in pairs:
            p = jnp.exp2((new_scores[r, j] - tops[r, j]) * factor)
            total_sum = jnp.sum(lane_sums[r, j], axis=1, keepdims=True) + jnp.sum(
                p, axis=1, keepdims=True
            )
            o = totals[r, j] + jnp.dot(
                p.astype(bf16), vn_scr[r, j].astype(bf16), preferred_element_type=f32
            )
            o = o / total_sum
            for g in range(group):
                col = (j * group + g) * head_dim
                o_scr[r * steps : (r + 1) * steps, col : col + head_dim] = o[
                    g * steps : (g + 1) * steps
                ]
        result = o_scr[...].astype(bf16)
        for n in range(copies):
            out_ref[n] = result

    flops = 4 * row_count * kv_heads * queries * cache_len * head_dim
    return pl.pallas_call(
        kernel,
        out_shape=pltpu.VMEM((copies, lines, q_width), bf16),
        in_specs=[scalars, scalars] + [whole] * 7,
        out_specs=whole,
        scratch_shapes=[
            pltpu.VMEM((row_count, kv_heads, queries, head_dim), f32),
            pltpu.VMEM((row_count, kv_heads, fresh, head_dim), f32),
            pltpu.VMEM((row_count, kv_heads, fresh, head_dim), f32),
            pltpu.VMEM((kv_heads, queries, cache_len), f32),
            pltpu.VMEM((lines, q_width), f32),
        ],
        compiler_params=params(12),
        cost_estimate=pl.CostEstimate(
            flops=flops,
            bytes_accessed=4 * row_count * kv_heads * cache_len * head_dim,
            transcendentals=0,
        ),
        name="attention",
    )(
        lengths,
        finished,
        parts,
        scale,
        *[b.reshape(-1, head_dim) for b in biases],
        key_cache,
        value_cache,
    )


def project(core, gathered, weights, near, tp):
    sources, per, width = gathered.shape
    chips = sources // tp
    cores = len(weights)
    columns = weights[0].shape[1]

    def kernel(core_ref, a_ref, near_ref, *refs):
        far = refs[: cores - 1]
        out_ref, held, sems = refs[cores - 1], refs[cores : 2 * cores - 1], refs[-1]
        first = core_ref[0] == 0
        copies = []
        for t in range(tp):
            part = pl.ds(t * width, width)
            for c in range(cores - 1):
                copies.append(
                    pltpu.make_async_copy(far[c].at[part, :], held[c].at[part, :], sems.at[t])
                )
                copies[-1].start()
        lhs = [
            jnp.concatenate([a_ref[slot_of(n, t, near, tp)] for n in range(chips)], axis=0)
            for t in range(tp)
        ]
        accs = []
        for c in range(cores):
            acc = None
            for t in range(tp):
                source = near_ref
                if c:
                    copies[t].wait()
                    source = held[c - 1]
                part = jnp.dot(
                    lhs[t], source[t * width : (t + 1) * width, :], preferred_element_type=f32
                )
                acc = part if acc is None else acc + part
            accs.append(acc)
        if cores == 2:
            accs = [jnp.where(first, accs[0], accs[1]), jnp.where(first, accs[1], accs[0])]
        acc = jnp.concatenate(accs, axis=1).astype(bf16)
        for n in range(chips):
            for t in range(tp):
                out_ref[slot_of(n, t, near, tp)] = acc[n * per : (n + 1) * per]

    return pl.pallas_call(
        kernel,
        out_shape=pltpu.VMEM((sources, per, cores * columns), bf16),
        in_specs=[scalars, whole, whole] + [distant] * (cores - 1),
        out_specs=whole,
        scratch_shapes=[pltpu.VMEM(w.shape, w.dtype) for w in weights[1:]]
        + [pltpu.SemaphoreType.DMA((tp,))],
        compiler_params=params(8),
        cost_estimate=pl.CostEstimate(
            flops=2 * chips * per * tp * width * cores * columns,
            bytes_accessed=2 * tp * width * cores * columns,
            transcendentals=0,
        ),
        name="project",
    )(core, gathered, *weights)


def finish(finished, arrived, hidden_tiles, shape, cores, near, tp):
    sources, lines, wide = arrived.shape
    step_count, row_count, model_width = shape
    chips = sources // tp
    width = wide // cores

    def kernel(finished_ref, a_ref, h_ref, out_ref, y_scr, out_scr, sems):
        line = lax.broadcasted_iota(jnp.int32, (lines, 128), 0)
        done = jnp.zeros((lines, 128), jnp.int32)
        for r in range(row_count):
            done = jnp.where(line // step_count == r, finished_ref[r], done)
        copies = []
        span = cores * tp * width
        for n in range(chips):
            for c, t in itertools.product(range(cores), range(tp)):
                for b in range(width // 128):
                    tile = ((n * cores + c) * tp + t) * (width // 128) + b
                    start = c * width + b * 128
                    moved = a_ref[slot_of(n, t, near, tp), :, start : start + 128].astype(f32)
                    hidden = h_ref[tile]
                    y_scr[tile] = jnp.where(done != 0, hidden, hidden + moved)
            for s in range(step_count):
                for b in range(n * span // 128, (n + 1) * span // 128):
                    out_scr[s, :, b * 128 : (b + 1) * 128] = y_scr[
                        b, pl.ds(s, row_count, stride=step_count), :
                    ].astype(bf16)
            part = pl.ds(n * span, span)
            copies.append(
                pltpu.make_async_copy(
                    out_scr.at[:, :, part], out_ref.at[:, :, part], sems.at[n]
                )
            )
            copies[-1].start()
        for copy in copies:
            copy.wait()

    return pl.pallas_call(
        kernel,
        out_shape=jax.ShapeDtypeStruct(shape, bf16),
        in_specs=[scalars, whole, whole],
        out_specs=distant,
        scratch_shapes=[
            pltpu.VMEM(hidden_tiles.shape, f32),
            pltpu.VMEM(shape, bf16),
            pltpu.SemaphoreType.DMA((chips,)),
        ],
        compiler_params=params(4),
        name="finish",
    )(finished, arrived, hidden_tiles)


def shards(
    hidden_in,
    norm_gain,
    w_query,
    key_weight_matrix,
    value_weight_matrix,
    bias_query,
    key_bias_vector,
    value_bias_vector,
    w_out,
    key_cache,
    value_cache,
    lengths,
    finished,
):
    step_count, row_count, model_width = hidden_in.shape
    lines = step_count * row_count
    head_dim = key_cache.shape[3]
    near = lax.axis_size("near")
    chips = lax.axis_size("far") * near
    chip_axes = ("far", "near")
    chip = lax.axis_index(chip_axes)
    cores = lax.axis_size("core")
    tp = lax.axis_size("tp")
    core = lax.axis_index("core")
    tp_index = lax.axis_index("tp")
    width = model_width // (chips * cores * tp)
    plane = ("far", "tp", "near")
    swap = [(i, cores - 1 - i) for i in range(cores)]

    def both(weight):
        return [weight] + ([lax.ppermute(weight, "core", swap)] if cores == 2 else [])

    queries_w = both(w_query)
    keys_w = both(key_weight_matrix)
    values_w = both(value_weight_matrix)

    core_place = core.astype(jnp.int32).reshape(1)
    tp_place = tp_index.astype(jnp.int32).reshape(1)
    chip_place = chip.astype(jnp.int32).reshape(1)
    if width % 128 == 0:
        *mine, scale, hidden_tiles, held_query = prepare(
            core_place, tp_place, chip_place, hidden_in, norm_gain, w_query, chips, cores, tp
        )
    else:
        by_row = jnp.transpose(hidden_in, (1, 0, 2)).reshape(lines, model_width).astype(f32)
        blocked = (by_row * norm_gain.astype(f32)).astype(bf16)
        blocked = blocked.reshape(lines, chips, cores, tp, width)
        mine = lax.dynamic_index_in_dim(blocked, tp_index, 3, keepdims=False)
        if cores == 2:
            mine = jnp.where(core == 0, mine, mine[:, :, ::-1])
        mine = jnp.transpose(mine, (1, 2, 0, 3)).reshape(chips, cores * lines, width)
        mine = [
            lax.dynamic_index_in_dim(mine, other_chip(chip, m, chips), 0, keepdims=False)
            for m in range(chips)
        ]
        scale = lax.rsqrt(jnp.mean(by_row * by_row, axis=-1, keepdims=True) + norm_eps)
        scale = jnp.broadcast_to(scale, (lines, 128))
    columns = []
    for m in range(chips):
        pairs = [(i, other_chip(i, m, chips)) for i in range(chips)]
        still = all(i == j for i, j in pairs)
        columns.append(mine[m] if still else lax.ppermute(mine[m], chip_axes, pairs))
    if width % 128 == 0:
        held = (held_query,) + tuple(staged((key_weight_matrix, value_weight_matrix), mine[0]))
    else:
        held = staged((w_query, key_weight_matrix, value_weight_matrix), mine[0])
    weights = [held] + list(zip(queries_w, keys_w, values_w))[1:]
    partials = qkv_partials(chip_place, columns, weights, near, tp, (key_cache, value_cache))
    parts = lax.all_to_all(partials, plane, split_axis=0, concat_axis=0, tiled=True)
    late_out, parts = lax.optimization_barrier((w_out, parts))
    outs_w = both(late_out)
    block = min(key_cache.shape[2], 8192)
    attended = attention(
        lengths,
        finished,
        parts,
        scale,
        (bias_query, key_bias_vector, value_bias_vector),
        key_cache,
        value_cache,
        chips * tp,
        block,
    )
    gathered = lax.all_to_all(attended, plane, split_axis=0, concat_axis=0, tiled=True)
    product = project(core_place, gathered, outs_w, near, tp)
    arrived = lax.all_to_all(product, plane, split_axis=0, concat_axis=0, tiled=True)
    if width % 128 == 0:
        return finish(finished, arrived, hidden_tiles, hidden_in.shape, cores, near, tp)
    arrived = arrived.reshape(chips // near, tp, near, row_count, step_count, cores, width)
    projected = jnp.transpose(arrived, (4, 3, 0, 2, 5, 1, 6)).reshape(
        step_count, row_count, model_width
    )
    hidden = hidden_in.astype(f32)
    layer_out = jnp.where(finished[None, :, None] != 0, hidden, hidden + projected.astype(f32))
    return layer_out.astype(bf16)


def solution(mesh):
    gen = mesh.shape["gen"]
    cores = 2 if gen % 2 == 0 else 1
    chips = gen // cores
    near = 2 if chips % 2 == 0 else 1
    split = Mesh(
        mesh.devices.reshape(chips // near, near, cores, mesh.shape["tp"]),
        ("far", "near", "core", "tp"),
    )
    rows = ("far", "near", "core")
    every = rows + ("tp",)
    placed = (
        P(None, rows, None),
        P(),
        P(every, None),
        P(every, None),
        P(every, None),
        P("tp"),
        P("tp"),
        P("tp"),
        P(None, every),
        P(rows, "tp", None, None),
        P(rows, "tp", None, None),
        P(rows),
        P(rows),
    )
    return jax.shard_map(
        shards, mesh=split, in_specs=placed, out_specs=P(None, rows, None), check_vma=False
    )
```

```python
import itertools
import math

import jax
import jax.numpy as jnp
from jax import lax
from jax.experimental import pallas as pl
from jax.experimental.pallas import tpu as pltpu
from jax.sharding import Mesh
from jax.sharding import PartitionSpec as P

norm_eps = 1e-06
rope_base = 1000000.0
masked_score = -1e30
bf16 = jnp.bfloat16
f32 = jnp.float32


whole = pl.BlockSpec(memory_space=pltpu.VMEM)
scalars = pl.BlockSpec(memory_space=pltpu.SMEM)
distant = pl.BlockSpec(memory_space=pltpu.HBM)


def far_away(array):
    return pltpu.with_memory_space_constraint(array, pltpu.HBM)


def params(mib):
    return pltpu.CompilerParams(vmem_limit_bytes=mib << 20)


def other_chip(chip, m, chips):
    if chips & (chips - 1) == 0:
        return chip ^ m
    return (m - chip) % chips


def slot_of(n, t, near, tp):
    return ((n // near) * tp + t) * near + n % near


def prepare(core, tp_index, chip, hidden_in, norm_gain, w_query, chips, cores, tp):
    step_count, row_count, model_width = hidden_in.shape
    lines = step_count * row_count
    width = model_width // (chips * cores * tp)

    def kernel(core_ref, tp_ref, chip_ref, h_hbm, g_hbm, w_hbm, *refs):
        mine_refs, scale_ref, x_ref, w_ref = refs[:chips], *refs[chips : chips + 3]
        h_ref, g_ref, g_scr, sems = refs[chips + 3 :]
        copies = [
            pltpu.make_async_copy(h_hbm, h_ref, sems.at[0]),
            pltpu.make_async_copy(g_hbm, g_ref, sems.at[1]),
            pltpu.make_async_copy(w_hbm, w_ref, sems.at[2]),
        ]
        for copy in copies:
            copy.start()
        for copy in copies[:2]:
            copy.wait()
        for s in range(step_count):
            for b in range(model_width // 128):
                x_ref[b, pl.ds(s, row_count, stride=step_count), :] = h_ref[
                    s, :, b * 128 : (b + 1) * 128
                ].astype(f32)
        g_scr[...] = g_ref[...].astype(f32)
        own = core_ref[0]
        for m in range(chips):
            n = other_chip(chip_ref[0], m, chips)
            for c in range(cores):
                at = own if c == 0 else 1 - own
                block = ((n * cores + at) * tp + tp_ref[0]) * (width // 128)
                for b in range(width // 128):
                    x = x_ref[block + b] * g_scr[pl.ds(block + b, 1), :]
                    mine_refs[m][c * lines : (c + 1) * lines, b * 128 : (b + 1) * 128] = x.astype(
                        bf16
                    )
        square = jnp.zeros((lines, 128), f32)
        for b in range(model_width // 128):
            square = square + x_ref[b] * x_ref[b]
        mean = jnp.sum(square, axis=1, keepdims=True) * (1.0 / model_width)
        scale_ref[...] = jnp.broadcast_to(lax.rsqrt(mean + norm_eps), (lines, 128))
        copies[2].wait()

    return pl.pallas_call(
        kernel,
        out_shape=(jax.ShapeDtypeStruct((cores * lines, width), bf16),) * chips
        + (
            jax.ShapeDtypeStruct((lines, 128), f32),
            pltpu.VMEM((model_width // 128, lines, 128), f32),
            pltpu.VMEM(w_query.shape, bf16),
        ),
        in_specs=[scalars, scalars, scalars, distant, distant, distant],
        out_specs=(whole,) * (chips + 3),
        scratch_shapes=[
            pltpu.VMEM(hidden_in.shape, bf16),
            pltpu.VMEM((model_width // 128, 128), bf16),
            pltpu.VMEM((model_width // 128, 128), f32),
            pltpu.SemaphoreType.DMA((3,)),
        ],
        compiler_params=params(4),
        name="prepare",
    )(
        core,
        tp_index,
        chip,
        far_away(hidden_in),
        far_away(norm_gain.reshape(model_width // 128, 128)),
        far_away(w_query),
    )


def staged(arrays, after):
    count = len(arrays)

    def kernel(*refs):
        sources, outs, sems = refs[:count], refs[count + 1 : 2 * count + 1], refs[-1]
        copies = [pltpu.make_async_copy(sources[i], outs[i], sems.at[i]) for i in range(count)]
        for copy in copies:
            copy.start()
        for copy in copies:
            copy.wait()

    return pl.pallas_call(
        kernel,
        out_shape=tuple(pltpu.VMEM(a.shape, a.dtype) for a in arrays),
        in_specs=[distant] * count + [pl.BlockSpec(memory_space=pl.ANY)],
        out_specs=(whole,) * count,
        scratch_shapes=[pltpu.SemaphoreType.DMA((count,))],
        compiler_params=params(1),
        cost_estimate=pl.CostEstimate(
            flops=0, bytes_accessed=sum(math.prod(a.shape) * 2 for a in arrays), transcendentals=0
        ),
        name="stage_weights",
    )(*[far_away(a) for a in arrays], after)


def qkv_partials(chip, columns, weights, near, tp, later):
    chips = len(columns)
    depth, width = columns[0].shape
    cores = len(weights)
    per = depth // cores
    rows = chips * per
    sizes = [w.shape[1] // tp for w in weights[0]]
    total = sum(sizes)
    flat = [w for group in weights for w in group]

    def kernel(chip_ref, *refs):
        x_refs, w_refs, out_ref = refs[:chips], refs[chips : chips + len(flat)], refs[-1]
        lhs = [
            jnp.concatenate([x[c * per : (c + 1) * per] for x in x_refs], axis=0)
            for c in range(cores)
        ]
        places = [other_chip(chip_ref[0], m, chips) for m in range(chips)]
        for t in range(tp):
            slots = [slot_of(n, t, near, tp) for n in places]
            start = 0
            for kind, size in enumerate(sizes):
                acc = None
                for c in range(cores):
                    w = w_refs[c * 3 + kind][:, t * size : (t + 1) * size]
                    part = jnp.dot(lhs[c], w, preferred_element_type=f32)
                    acc = part if acc is None else acc + part
                acc = acc.astype(bf16)
                for m in range(chips):
                    out_ref[slots[m], :, start : start + size] = acc[m * per : (m + 1) * per]
                start += size

    return pl.pallas_call(
        kernel,
        out_shape=pltpu.VMEM((chips * tp, per, total), bf16),
        in_specs=[scalars] + [whole] * (chips + len(flat)) + [distant] * len(later),
        out_specs=whole,
        compiler_params=params(6),
        cost_estimate=pl.CostEstimate(
            flops=2 * cores * rows * width * total * tp,
            bytes_accessed=2 * cores * width * total * tp,
            transcendentals=0,
        ),
        name="qkv_partials",
    )(chip, *columns, *flat, *[far_away(x) for x in later])


def attention(lengths, finished, parts, scale, biases, key_cache, value_cache, copies, block):
    sources, lines, total = parts.shape
    row_count, kv_heads, cache_len, head_dim = key_cache.shape
    steps = lines // row_count
    kv_width = kv_heads * head_dim
    q_width = total - 2 * kv_width
    heads = q_width // head_dim
    group = heads // kv_heads
    queries = group * steps
    fresh = 8
    small = min(block, 1024)
    sizes = [block >> i for i in range(3) if block >> i > small]
    factor = math.log2(math.e) / math.sqrt(head_dim)
    pairs = [(r, j) for r in range(row_count) for j in range(kv_heads)]

    def kernel(length_ref, finished_ref, p_ref, scale_ref, bq_ref, bk_ref, bv_ref, k_ref, v_ref,
               out_ref, q_scr, kn_scr, vn_scr, s_scr, o_scr):
        lives = [
            jnp.where(finished_ref[r] != 0, 0, length_ref[r]) for r in range(row_count)
        ]
        plans = []
        for length in lives:
            offset = length * 0
            plan = []
            for size in sizes:
                count = (length - offset) // size
                plan.append((offset, count, size, False))
                offset = offset + count * size
            plan.append((offset, (length - offset + small - 1) // small, small, True))
            plans.append(plan)

        def over(plan, step, carry):
            for offset, count, size, masked in plan:

                def one(i, carry, offset=offset, size=size, masked=masked):
                    return step(pl.multiple_of(offset + i * size, small), size, masked, carry)

                carry = lax.fori_loop(0, count, one, carry)
            return carry

        scale = scale_ref[...]
        line = lax.broadcasted_iota(jnp.int32, (lines, head_dim), 0)
        lane = lax.broadcasted_iota(jnp.int32, (lines, head_dim), 1)
        position = line % steps
        for r in range(row_count):
            position = position + jnp.where(line // steps == r, length_ref[r], 0)
        half = head_dim // 2
        pair = (lane % half).astype(f32)
        frequency = jnp.exp(pair * (-2.0 * math.log(rope_base) / head_dim))
        angles = position.astype(f32) * frequency
        cos = jnp.cos(angles)
        sin = jnp.where(lane < half, -1.0, 1.0) * jnp.sin(angles)

        def summed(start, bias_row):
            terms = [p_ref[i, :, start : start + head_dim].astype(f32) for i in range(sources)]
            while len(terms) > 1:
                terms = [sum(terms[i : i + 2]) for i in range(0, len(terms), 2)]
            return terms[0] * scale + bias_row.astype(f32)

        def rotated(start, bias_row):
            head = summed(start, bias_row)
            return head * cos + pltpu.roll(head, half, 1) * sin

        kn_scr[...] = jnp.zeros_like(kn_scr)
        vn_scr[...] = jnp.zeros_like(vn_scr)
        for h in range(heads):
            q = rotated(h * head_dim, bq_ref[h : h + 1, :])
            for r in range(row_count):
                g = h % group
                q_scr[r, h // group, g * steps : (g + 1) * steps, :] = q[r * steps : (r + 1) * steps]
        for j in range(kv_heads):
            k = rotated(q_width + j * head_dim, bk_ref[j : j + 1, :])
            v = summed(q_width + kv_width + j * head_dim, bv_ref[j : j + 1, :])
            for r in range(row_count):
                kn_scr[r, j, 0:steps, :] = k[r * steps : (r + 1) * steps]
                vn_scr[r, j, 0:steps, :] = v[r * steps : (r + 1) * steps]
        step_of = lax.broadcasted_iota(jnp.int32, (queries, fresh), 0) % steps
        allowed = lax.broadcasted_iota(jnp.int32, (queries, fresh), 1) <= step_of
        nt = (((1,), (1,)), ((), ()))
        qs = {}
        new_scores = {}
        new_tops = {}
        for r, j in pairs:
            qs[r, j] = q_scr[r, j].astype(bf16)
            s = lax.dot_general(
                qs[r, j], kn_scr[r, j].astype(bf16), nt, preferred_element_type=f32
            )
            new_scores[r, j] = jnp.where(allowed, s, masked_score)
            new_tops[r, j] = jnp.max(new_scores[r, j], axis=1, keepdims=True)
        tops = {}
        lane_sums = {}
        totals = {}
        for r in range(row_count):

            def scores(start, size, masked, most):
                out = []
                for j in range(kv_heads):
                    s = lax.dot_general(
                        qs[r, j], k_ref[r, j, pl.ds(start, size), :], nt, preferred_element_type=f32
                    )
                    if masked:
                        place = start + lax.broadcasted_iota(jnp.int32, (queries, size), 1)
                        s = jnp.where(place < lives[r], s, masked_score)
                    s_scr[j, :, pl.ds(start, size)] = s
                    top = most[j]
                    for b in range(size // 128):
                        top = jnp.maximum(top, s[:, b * 128 : (b + 1) * 128])
                    out.append(top)
                return tuple(out)

            most = tuple(jnp.full((queries, 128), masked_score, f32) for _ in range(kv_heads))
            most = over(plans[r], scores, most)
            for j in range(kv_heads):
                tops[r, j] = jnp.maximum(
                    jnp.max(most[j], axis=1, keepdims=True), new_tops[r, j]
                )

            def gather(start, size, masked, carry):
                lanes, accs = carry
                new_lanes = []
                new_accs = []
                for j in range(kv_heads):
                    p = jnp.exp2((s_scr[j, :, pl.ds(start, size)] - tops[r, j]) * factor)
                    lane_sum = lanes[j]
                    for b in range(size // 128):
                        lane_sum = lane_sum + p[:, b * 128 : (b + 1) * 128]
                    new_lanes.append(lane_sum)
                    new_accs.append(
                        accs[j]
                        + jnp.dot(
                            p.astype(bf16),
                            v_ref[r, j, pl.ds(start, size), :],
                            preferred_element_type=f32,
                        )
                    )
                return tuple(new_lanes), tuple(new_accs)

            carry = (
                tuple(jnp.zeros((queries, 128), f32) for _ in range(kv_heads)),
                tuple(jnp.zeros((queries, head_dim), f32) for _ in range(kv_heads)),
            )
            carry = over(plans[r], gather, carry)
            for j in range(kv_heads):
                lane_sums[r, j] = carry[0][j]
                totals[r, j] = carry[1][j]
        for r, j in pairs:
            p = jnp.exp2((new_scores[r, j] - tops[r, j]) * factor)
            total_sum = jnp.sum(lane_sums[r, j], axis=1, keepdims=True) + jnp.sum(
                p, axis=1, keepdims=True
            )
            o = totals[r, j] + jnp.dot(
                p.astype(bf16), vn_scr[r, j].astype(bf16), preferred_element_type=f32
            )
            o = o / total_sum
            for g in range(group):
                col = (j * group + g) * head_dim
                o_scr[r * steps : (r + 1) * steps, col : col + head_dim] = o[
                    g * steps : (g + 1) * steps
                ]
        result = o_scr[...].astype(bf16)
        for n in range(copies):
            out_ref[n] = result

    flops = 4 * row_count * kv_heads * queries * cache_len * head_dim
    return pl.pallas_call(
        kernel,
        out_shape=pltpu.VMEM((copies, lines, q_width), bf16),
        in_specs=[scalars, scalars] + [whole] * 7,
        out_specs=whole,
        scratch_shapes=[
            pltpu.VMEM((row_count, kv_heads, queries, head_dim), f32),
            pltpu.VMEM((row_count, kv_heads, fresh, head_dim), f32),
            pltpu.VMEM((row_count, kv_heads, fresh, head_dim), f32),
            pltpu.VMEM((kv_heads, queries, cache_len), f32),
            pltpu.VMEM((lines, q_width), f32),
        ],
        compiler_params=params(12),
        cost_estimate=pl.CostEstimate(
            flops=flops,
            bytes_accessed=4 * row_count * kv_heads * cache_len * head_dim,
            transcendentals=0,
        ),
        name="attention",
    )(
        lengths,
        finished,
        parts,
        scale,
        *[b.reshape(-1, head_dim) for b in biases],
        key_cache,
        value_cache,
    )


def project(core, gathered, weights, near, tp):
    sources, per, width = gathered.shape
    chips = sources // tp
    cores = len(weights)
    columns = weights[0].shape[1]

    def kernel(core_ref, a_ref, near_ref, *refs):
        far = refs[: cores - 1]
        out_ref, held, sems = refs[cores - 1], refs[cores : 2 * cores - 1], refs[-1]
        first = core_ref[0] == 0
        copies = []
        for t in range(tp):
            part = pl.ds(t * width, width)
            for c in range(cores - 1):
                copies.append(
                    pltpu.make_async_copy(far[c].at[part, :], held[c].at[part, :], sems.at[t])
                )
                copies[-1].start()
        lhs = [
            jnp.concatenate([a_ref[slot_of(n, t, near, tp)] for n in range(chips)], axis=0)
            for t in range(tp)
        ]
        accs = []
        for c in range(cores):
            acc = None
            for t in range(tp):
                source = near_ref
                if c:
                    copies[t].wait()
                    source = held[c - 1]
                part = jnp.dot(
                    lhs[t], source[t * width : (t + 1) * width, :], preferred_element_type=f32
                )
                acc = part if acc is None else acc + part
            accs.append(acc)
        if cores == 2:
            accs = [jnp.where(first, accs[0], accs[1]), jnp.where(first, accs[1], accs[0])]
        acc = jnp.concatenate(accs, axis=1).astype(bf16)
        for n in range(chips):
            for t in range(tp):
                out_ref[slot_of(n, t, near, tp)] = acc[n * per : (n + 1) * per]

    return pl.pallas_call(
        kernel,
        out_shape=pltpu.VMEM((sources, per, cores * columns), bf16),
        in_specs=[scalars, whole, whole] + [distant] * (cores - 1),
        out_specs=whole,
        scratch_shapes=[pltpu.VMEM(w.shape, w.dtype) for w in weights[1:]]
        + [pltpu.SemaphoreType.DMA((tp,))],
        compiler_params=params(8),
        cost_estimate=pl.CostEstimate(
            flops=2 * chips * per * tp * width * cores * columns,
            bytes_accessed=2 * tp * width * cores * columns,
            transcendentals=0,
        ),
        name="project",
    )(core, gathered, *weights)


def finish(finished, arrived, hidden_tiles, shape, cores, near, tp):
    sources, lines, wide = arrived.shape
    step_count, row_count, model_width = shape
    chips = sources // tp
    width = wide // cores

    def kernel(finished_ref, a_ref, h_ref, out_ref, y_scr, out_scr, sems):
        line = lax.broadcasted_iota(jnp.int32, (lines, 128), 0)
        done = jnp.zeros((lines, 128), jnp.int32)
        for r in range(row_count):
            done = jnp.where(line // step_count == r, finished_ref[r], done)
        copies = []
        span = cores * tp * width
        for n in range(chips):
            for c, t in itertools.product(range(cores), range(tp)):
                for b in range(width // 128):
                    tile = ((n * cores + c) * tp + t) * (width // 128) + b
                    start = c * width + b * 128
                    moved = a_ref[slot_of(n, t, near, tp), :, start : start + 128].astype(f32)
                    hidden = h_ref[tile]
                    y_scr[tile] = jnp.where(done != 0, hidden, hidden + moved)
            for s in range(step_count):
                for b in range(n * span // 128, (n + 1) * span // 128):
                    out_scr[s, :, b * 128 : (b + 1) * 128] = y_scr[
                        b, pl.ds(s, row_count, stride=step_count), :
                    ].astype(bf16)
            part = pl.ds(n * span, span)
            copies.append(
                pltpu.make_async_copy(
                    out_scr.at[:, :, part], out_ref.at[:, :, part], sems.at[n]
                )
            )
            copies[-1].start()
        for copy in copies:
            copy.wait()

    return pl.pallas_call(
        kernel,
        out_shape=jax.ShapeDtypeStruct(shape, bf16),
        in_specs=[scalars, whole, whole],
        out_specs=distant,
        scratch_shapes=[
            pltpu.VMEM(hidden_tiles.shape, f32),
            pltpu.VMEM(shape, bf16),
            pltpu.SemaphoreType.DMA((chips,)),
        ],
        compiler_params=params(4),
        name="finish",
    )(finished, arrived, hidden_tiles)


def shards(
    hidden_in,
    norm_gain,
    w_query,
    key_weight_matrix,
    value_weight_matrix,
    bias_query,
    key_bias_vector,
    value_bias_vector,
    w_out,
    key_cache,
    value_cache,
    lengths,
    finished,
):
    step_count, row_count, model_width = hidden_in.shape
    lines = step_count * row_count
    head_dim = key_cache.shape[3]
    near = lax.axis_size("near")
    chips = lax.axis_size("far") * near
    chip_axes = ("far", "near")
    chip = lax.axis_index(chip_axes)
    cores = lax.axis_size("core")
    tp = lax.axis_size("tp")
    core = lax.axis_index("core")
    tp_index = lax.axis_index("tp")
    width = model_width // (chips * cores * tp)
    plane = ("far", "tp", "near")
    swap = [(i, cores - 1 - i) for i in range(cores)]

    def both(weight):
        return [weight] + ([lax.ppermute(weight, "core", swap)] if cores == 2 else [])

    queries_w = both(w_query)
    keys_w = both(key_weight_matrix)
    values_w = both(value_weight_matrix)

    core_place = core.astype(jnp.int32).reshape(1)
    tp_place = tp_index.astype(jnp.int32).reshape(1)
    chip_place = chip.astype(jnp.int32).reshape(1)
    if width % 128 == 0:
        *mine, scale, hidden_tiles, held_query = prepare(
            core_place, tp_place, chip_place, hidden_in, norm_gain, w_query, chips, cores, tp
        )
    else:
        by_row = jnp.transpose(hidden_in, (1, 0, 2)).reshape(lines, model_width).astype(f32)
        blocked = (by_row * norm_gain.astype(f32)).astype(bf16)
        blocked = blocked.reshape(lines, chips, cores, tp, width)
        mine = lax.dynamic_index_in_dim(blocked, tp_index, 3, keepdims=False)
        if cores == 2:
            mine = jnp.where(core == 0, mine, mine[:, :, ::-1])
        mine = jnp.transpose(mine, (1, 2, 0, 3)).reshape(chips, cores * lines, width)
        mine = [
            lax.dynamic_index_in_dim(mine, other_chip(chip, m, chips), 0, keepdims=False)
            for m in range(chips)
        ]
        scale = lax.rsqrt(jnp.mean(by_row * by_row, axis=-1, keepdims=True) + norm_eps)
        scale = jnp.broadcast_to(scale, (lines, 128))
    columns = []
    for m in range(chips):
        pairs = [(i, other_chip(i, m, chips)) for i in range(chips)]
        still = all(i == j for i, j in pairs)
        columns.append(mine[m] if still else lax.ppermute(mine[m], chip_axes, pairs))
    if width % 128 == 0:
        held = (held_query,) + tuple(staged((key_weight_matrix, value_weight_matrix), mine[0]))
    else:
        held = staged((w_query, key_weight_matrix, value_weight_matrix), mine[0])
    weights = [held] + list(zip(queries_w, keys_w, values_w))[1:]
    partials = qkv_partials(chip_place, columns, weights, near, tp, (key_cache, value_cache))
    parts = lax.all_to_all(partials, plane, split_axis=0, concat_axis=0, tiled=True)
    late_out, parts = lax.optimization_barrier((w_out, parts))
    outs_w = both(late_out)
    block = min(key_cache.shape[2], 8192)
    attended = attention(
        lengths,
        finished,
        parts,
        scale,
        (bias_query, key_bias_vector, value_bias_vector),
        key_cache,
        value_cache,
        chips * tp,
        block,
    )
    gathered = lax.all_to_all(attended, plane, split_axis=0, concat_axis=0, tiled=True)
    product = project(core_place, gathered, outs_w, near, tp)
    arrived = lax.all_to_all(product, plane, split_axis=0, concat_axis=0, tiled=True)
    if width % 128 == 0:
        return finish(finished, arrived, hidden_tiles, hidden_in.shape, cores, near, tp)
    arrived = arrived.reshape(chips // near, tp, near, row_count, step_count, cores, width)
    projected = jnp.transpose(arrived, (4, 3, 0, 2, 5, 1, 6)).reshape(
        step_count, row_count, model_width
    )
    hidden = hidden_in.astype(f32)
    layer_out = jnp.where(finished[None, :, None] != 0, hidden, hidden + projected.astype(f32))
    return layer_out.astype(bf16)


def solution(mesh):
    gen = mesh.shape["gen"]
    cores = 2 if gen % 2 == 0 else 1
    chips = gen // cores
    near = 2 if chips % 2 == 0 else 1
    split = Mesh(
        mesh.devices.reshape(chips // near, near, cores, mesh.shape["tp"]),
        ("far", "near", "core", "tp"),
    )
    rows = ("far", "near", "core")
    every = rows + ("tp",)
    placed = (
        P(None, rows, None),
        P(),
        P(every, None),
        P(every, None),
        P(every, None),
        P("tp"),
        P("tp"),
        P("tp"),
        P(None, every),
        P(rows, "tp", None, None),
        P(rows, "tp", None, None),
        P(rows),
        P(rows),
    )
    return jax.shard_map(
        shards, mesh=split, in_specs=placed, out_specs=P(None, rows, None), check_vma=False
    )
```
